32 devices in a mesh: member: 8 (over y, x, core), lat: 4 (over z).
Axes of the slice: x: 2, y: 2, z: 4, core: 2. Of those that a mesh axis runs over, the one named last changes fastest.
Arguments:
- state: float32 [32, 32, 8, 256], P('member', 'lat'), may hold values from -6 to 6
- zonal_wind: float32 [32, 8, 256], P('lat'), may hold values from -5 to 5
- meridional_wind: float32 [32, 8, 256], P('lat'), may hold values from -5 to 5
- obs_cell: int32 [32, 8, 128], P('lat'), may hold values from 0 to 255
- obs_value: float32 [32, 8, 128], P('lat'), may hold values from -10 to 10
- obs_weight: float32 [32, 8, 128], P('lat'), may hold values from 1 to 1024
Outputs:
- analysis: float32 [32, 32, 8, 256], P('member', 'lat')
The draws below stay inside these ranges and needn't reach their ends.
All inputs are finite; a program needn't handle non-finite values.
Results may differ from the reference program's by a relative error of at most 0.00014.
Values sent between devices are 32-bit elements; how exact they have to be, the bound alone decides.
No kernel may reach another device: no remote copies, remote signals or barrier semaphores. Data moves between devices by JAX's collectives and lax.ppermute only.
A program may use at most 64 MiB of HBM per device.

```python
import math
import jax
import jax.numpy as jnp
from jax import lax

MEMBERS = 32
NLAT = 32
LEV = 8
NLON = 256
OBS = 128
SWEEPS = 3


def set_ends(array, stream_key, least, high):
    extent = array.shape
    index_at = [jax.random.randint(jax.random.fold_in(stream_key, axis), (), 0, extent[axis]) for axis in range(len(extent))]
    array = array.at[tuple(index_at)].set(least)
    longest = extent.index(max(extent))
    index_at[longest] = (index_at[longest] + 1) % extent[longest]
    return array.at[tuple(index_at)].set(high)


def levels(key, shape, split, least, high):
    loudness = 1.0
    for position, blocks in split:
        draws = jax.random.uniform(jax.random.fold_in(jax.random.fold_in(key, 6), position), (blocks,), jnp.float32, least / len(split), high / len(split))
        loudness = loudness * jnp.repeat(jnp.exp(draws), shape[position] // blocks).reshape((-1,) + (1,) * (len(shape) - 1 - position))
    return loudness


def gaussian(rng, dims, spread, limit, cuts=(), held_as=jnp.bfloat16):
    gain = levels(rng, dims, cuts, -0.22, 0.18) if cuts else 1.0
    array = jax.random.normal(rng, dims, jnp.float32) * spread * gain
    return jnp.minimum(jnp.maximum(array, -limit), limit).astype(held_as)


def setup_inputs(seed: int = 0) -> dict:
    splits = jax.random.split(jax.random.key(seed), 7)
    return {
        "state": gaussian(splits[0], (MEMBERS, NLAT, LEV, NLON), 1.0, 6.0, ((0, 8), (1, 4)), jnp.float32),
        "zonal_wind": gaussian(splits[1], (NLAT, LEV, NLON), 1.0, 5.0, ((0, 4),), jnp.float32),
        "meridional_wind": gaussian(splits[2], (NLAT, LEV, NLON), 1.0, 5.0, ((0, 4),), jnp.float32),
        "obs_cell": set_ends(jax.random.randint(splits[3], (NLAT, LEV, OBS), 0, NLON), jax.random.fold_in(splits[3], 1), 0, NLON - 1).astype(jnp.int32),
        "obs_value": gaussian(splits[4], (NLAT, LEV, OBS), 2.0, 10.0, ((0, 4),), jnp.float32),
        "obs_weight": jnp.clip(jnp.exp(math.log(1024.0) - 6.931472 * jax.random.uniform(splits[5], (NLAT, LEV, OBS), jnp.float32) ** levels(splits[5], (NLAT, LEV, OBS), ((0, 4),), -0.2, 0.2)), 1.0, 1024.0),
    }


step_size = 0.3

def advance(padded, zonal, meridional):
    middle = padded[:, 1:-1]
    north_row = padded[:, 2:]
    south_row = padded[:, :-2]
    east_cell = jnp.roll(middle, -1, axis=3)
    west_cell = jnp.roll(middle, 1, axis=3)
    return middle - step_size * ((zonal + middle) * (east_cell - west_cell) * 0.5 + meridional * (north_row - south_row) * 0.5)

def analyse(ensemble, observed, values, weights):
    highest = lax.Precision.HIGHEST
    count = ensemble.shape[0]
    obs_mean = lax.optimization_barrier(jnp.mean(observed, axis=0))
    perturb = observed - obs_mean
    innovation = values - obs_mean
    gram = jnp.einsum('kro,lro->rkl', perturb * weights, perturb, precision=highest)
    identity = jnp.eye(count, dtype=jnp.float32)
    system = gram + (count - 1.0) * identity
    frobenius = jnp.sqrt(lax.optimization_barrier(jnp.sum(system * system, axis=(1, 2))))
    iterate = system / frobenius[:, None, None]
    inverse = jnp.broadcast_to(identity, system.shape)
    for sweep in range(SWEEPS):
        product = jnp.einsum('rij,rjk->rik', inverse, iterate, precision=highest)
        factor = 1.5 * identity - 0.5 * product
        iterate = jnp.einsum('rij,rjk->rik', iterate, factor, precision=highest)
        inverse = jnp.einsum('rij,rjk->rik', factor, inverse, precision=highest)
    root = inverse / jnp.sqrt(frobenius)[:, None, None]
    covariance = jnp.einsum('rij,rjk->rik', root, root, precision=highest)
    projected = jnp.einsum('kro,ro->rk', perturb, weights * innovation, precision=highest)
    mean_weights = jnp.einsum('rkl,rl->rk', covariance, projected, precision=highest)
    transform = mean_weights[:, :, None] + jnp.sqrt(count - 1.0) * root
    state_mean = lax.optimization_barrier(jnp.mean(ensemble, axis=0))
    state_pert = ensemble - state_mean
    return state_mean + jnp.einsum('rkm,krn->mrn', transform, state_pert, precision=highest)

def reference(state, zonal_wind, meridional_wind, obs_cell, obs_value, obs_weight):
    count = state.shape[0]
    field = state
    for iteration in range(2):
        padded = jnp.pad(field, ((0, 0), (1, 1), (0, 0), (0, 0)))
        field = advance(padded, zonal_wind, meridional_wind)
    latitude_rows = jnp.transpose(field, (1, 0, 2, 3))

    def one_row(items):
        band_rows, cells, values, weights = items
        picked = jnp.take_along_axis(band_rows, jnp.broadcast_to(cells[None], (count,) + cells.shape), axis=2)
        return analyse(band_rows, picked, values, weights)
    result = lax.map(one_row, (latitude_rows, obs_cell, obs_value, obs_weight))
    return jnp.transpose(result, (1, 0, 2, 3))
```

```python
import functools

import jax
import jax.numpy as jnp
from jax import lax
from jax.experimental import pallas as pl
from jax.experimental.pallas import tpu as pltpu
from jax.sharding import PartitionSpec as P

SWEEPS = 3
step_size = 0.3
VM = pltpu.VMEM


def whole(n):
    return [pl.BlockSpec(memory_space=VM)] * n


def pair_rounds(count):
    def pairs(first):
        partner = list(range(count))
        for i in range(first, count - 1, 2):
            partner[i], partner[i + 1] = i + 1, i
        return [(i, partner[i]) for i in range(count)]

    return pairs(0), pairs(1)


def edge_message(state, zonal, meridional, at_high):
    members, rows, levels, lon = state.shape
    start = jnp.where(at_high, rows - 2, 0)
    row = jnp.where(at_high, rows - 1, 0)
    fields = lax.dynamic_slice_in_dim(state, start, 2, 1)
    winds = [lax.dynamic_slice_in_dim(w, row, 1, 0) for w in (zonal, meridional)]
    return jnp.concatenate([fields.reshape(members * 2, levels, lon), *winds], axis=0)


def advance(south, middle, north, zonal, meridional):
    lon = middle.shape[-1]
    axis = middle.ndim - 1
    east = pltpu.roll(middle, lon - 1, axis)
    west = pltpu.roll(middle, 1, axis)
    return middle - step_size * (
        (zonal + middle) * (east - west) * 0.5 + meridional * (north - south) * 0.5
    )


def forecast_kernel(where_ref, state_ref, e_ref, o_ref, zonal_ref, merid_ref, out_ref):
    members, rows, levels, lon = state_ref.shape
    even = where_ref[0] == 1
    has_low = where_ref[1].astype(jnp.float32)
    has_high = where_ref[2].astype(jnp.float32)

    def halo(i):
        e, o = e_ref[i], o_ref[i]
        low = jnp.where(even, o, e) * has_low
        high = jnp.where(even, e, o) * has_high
        return low, high

    z_low, z_high = halo(members * 2)
    m_low, m_high = halo(members * 2 + 1)
    zonal = [z_low] + [zonal_ref[r] for r in range(rows)] + [z_high]
    merid = [m_low] + [merid_ref[r] for r in range(rows)] + [m_high]
    for m in range(members):
        low0, high0 = halo(2 * m)
        low1, high1 = halo(2 * m + 1)
        q = [low0, low1] + [state_ref[m, r] for r in range(rows)] + [high0, high1]
        first = [
            advance(q[r], q[r + 1], q[r + 2], zonal[r], merid[r]) for r in range(rows + 2)
        ]
        for r in range(rows):
            out_ref[r, m] = advance(
                first[r], first[r + 1], first[r + 2], zonal[r + 1], merid[r + 1]
            )


def forecast(where, state, e_msg, o_msg, zonal, merid):
    members, rows, levels, lon = state.shape
    size = state.size
    return pl.pallas_call(
        forecast_kernel,
        out_shape=jax.ShapeDtypeStruct((rows, members, levels, lon), jnp.float32),
        in_specs=[pl.BlockSpec(memory_space=pltpu.SMEM)] + whole(5),
        out_specs=pl.BlockSpec(memory_space=VM),
        cost_estimate=pl.CostEstimate(
            flops=24 * size, bytes_accessed=8 * size, transcendentals=0
        ),
        name="forecast",
    )(where, state, e_msg, o_msg, zonal, merid)


def cells_kernel(cell_ref, value_ref, weight_ref, dsum_ref, vsum_ref):
    regions, obs = cell_ref.shape
    lon = dsum_ref.shape[1]
    weight = weight_ref[...]
    cell_t = cell_ref[...].T
    weight_t = weight.T
    value_t = (weight * value_ref[...]).T
    index = lax.broadcasted_iota(jnp.int32, (obs, lon), 1)
    for r in range(regions):
        hit = jnp.broadcast_to(cell_t[:, r : r + 1], (obs, lon)) == index
        w = jnp.broadcast_to(weight_t[:, r : r + 1], (obs, lon))
        v = jnp.broadcast_to(value_t[:, r : r + 1], (obs, lon))
        dsum_ref[r : r + 1, :] = jnp.sum(jnp.where(hit, w, 0.0), axis=0, keepdims=True)
        vsum_ref[r : r + 1, :] = jnp.sum(jnp.where(hit, v, 0.0), axis=0, keepdims=True)


def per_cell(cells, values, weights, lon):
    regions, obs = cells.shape
    shape = jax.ShapeDtypeStruct((regions, lon), jnp.float32)
    return pl.pallas_call(
        cells_kernel,
        out_shape=(shape, shape),
        in_specs=whole(3),
        out_specs=tuple(whole(2)),
        cost_estimate=pl.CostEstimate(
            flops=4 * regions * obs * lon,
            bytes_accessed=4 * (3 * regions * obs + 2 * regions * lon),
            transcendentals=0,
        ),
        name="per_cell",
    )(cells, values, weights)


def split(x):
    high = x.astype(jnp.bfloat16)
    low = (x - high.astype(jnp.float32)).astype(jnp.bfloat16)
    return high, low


def product(a, b, dims=((1,), (0,))):
    def dot(x, y):
        return lax.dot_general(x, y, (dims, ((), ())), preferred_element_type=jnp.float32)

    return dot(a[0], b[0]) + (dot(a[0], b[1]) + dot(a[1], b[0]))


def analysis_kernel(regions, ens_ref, dsum_ref, vsum_ref, out_ref):
    size, lon = ens_ref.shape
    count = size // regions

    def over_members(x):
        if regions == 1:
            return jnp.sum(x, axis=0, keepdims=True)
        return jnp.sum(x.reshape(count, regions, x.shape[-1]), axis=0)

    def spread(x):
        if regions == 1:
            return jnp.broadcast_to(x, (size, x.shape[-1]))
        x = jnp.broadcast_to(x[None], (count, regions, x.shape[-1]))
        return x.reshape(size, x.shape[-1])

    ens = ens_ref[...]
    dsum = dsum_ref[...]
    mean = over_members(ens) * (1.0 / count)
    pert = ens - spread(mean)
    pull = vsum_ref[...] - dsum * mean

    row = lax.broadcasted_iota(jnp.int32, (size, size), 0)
    col = lax.broadcasted_iota(jnp.int32, (size, size), 1)
    same = lax.rem(row, regions) == lax.rem(col, regions)
    one = jnp.where(row == col, 1.0, 0.0)

    pert_s = split(pert)
    gram = product(split(pert * spread(dsum)), pert_s, ((1,), (1,)))
    system = jnp.where(same, gram, 0.0) + (count - 1.0) * one
    total = over_members(jnp.sum(system * system, axis=1, keepdims=True))
    frob = jnp.sqrt(total)
    iterate = system * spread(1.0 / frob)
    iterate_s = split(iterate)
    inverse_s = None
    for sweep in range(SWEEPS):
        step = iterate if inverse_s is None else product(inverse_s, iterate_s)
        factor_s = split(1.5 * one - 0.5 * step)
        if sweep == SWEEPS - 1:
            break
        iterate_s = split(product(iterate_s, factor_s))
        inverse_s = factor_s if inverse_s is None else split(product(factor_s, inverse_s))
    part_s = split(product(inverse_s, pert_s))
    update = product(factor_s, part_s) * spread(lax.rsqrt(frob))
    gain = jnp.sum(update * spread(pull), axis=1, keepdims=True)
    shift = mean + over_members(update * gain)
    out_ref[...] = spread(shift) + jnp.sqrt(count - 1.0) * update


def analysis(ens, dsum, vsum):
    size, lon = ens.shape
    regions = dsum.shape[0]
    return pl.pallas_call(
        functools.partial(analysis_kernel, regions),
        out_shape=jax.ShapeDtypeStruct((size, lon), jnp.float32),
        in_specs=whole(3),
        out_specs=pl.BlockSpec(memory_space=VM),
        cost_estimate=pl.CostEstimate(
            flops=48 * size * size * lon, bytes_accessed=8 * size * lon, transcendentals=0
        ),
        name="analysis",
    )(ens, dsum, vsum)


def body(state, zonal_wind, meridional_wind, obs_cell, obs_value, obs_weight):
    members_dev, lat_dev, levels, longitudes = state.shape
    groups = lax.axis_size("member")
    bands = lax.axis_size("lat")
    regions = lat_dev * levels // groups
    count = members_dev * groups
    band = lax.axis_index("lat")
    even = lax.rem(band, 2) == 0

    first_round, second_round = pair_rounds(bands)
    e_msg = lax.ppermute(
        edge_message(state, zonal_wind, meridional_wind, even), "lat", first_round
    )
    o_msg = lax.ppermute(
        edge_message(state, zonal_wind, meridional_wind, jnp.logical_not(even)),
        "lat",
        second_round,
    )

    def mine(x):
        x = x.reshape(groups, regions, x.shape[-1])
        return lax.dynamic_index_in_dim(x, lax.axis_index("member"), 0, keepdims=False)

    dsum, vsum = per_cell(mine(obs_cell), mine(obs_value), mine(obs_weight), longitudes)

    where = jnp.stack([even, band > 0, band < bands - 1]).astype(jnp.int32)
    field = forecast(where, state, e_msg, o_msg, zonal_wind, meridional_wind)
    blocks = field.transpose(1, 0, 2, 3).reshape(members_dev, groups, regions, longitudes)
    ensemble = lax.all_to_all(
        blocks.transpose(1, 0, 2, 3), "member", split_axis=0, concat_axis=0, tiled=True
    )
    analysed = analysis(ensemble.reshape(count * regions, longitudes), dsum, vsum)
    returned = lax.all_to_all(
        analysed.reshape(groups, members_dev, regions, longitudes),
        "member",
        split_axis=0,
        concat_axis=0,
        tiled=True,
    )
    return returned.transpose(1, 0, 2, 3).reshape(state.shape)


def solution(mesh):
    in_specs = (
        P("member", "lat", None, None),
        P("lat", None, None),
        P("lat", None, None),
        P("lat", None, None),
        P("lat", None, None),
        P("lat", None, None),
    )
    out_specs = P("member", "lat", None, None)
    return jax.shard_map(body, mesh=mesh, in_specs=in_specs, out_specs=out_specs, check_vma=False)
```

```python
import functools

import jax
import jax.numpy as jnp
from jax import lax
from jax.experimental import pallas as pl
from jax.experimental.pallas import tpu as pltpu
from jax.sharding import PartitionSpec as P

SWEEPS = 3
step_size = 0.3
VM = pltpu.VMEM
SMALL = pltpu.CompilerParams(vmem_limit_bytes=12 * 2**20)


def whole(n):
    return [pl.BlockSpec(memory_space=VM)] * n


def pair_rounds(count):
    def pairs(first):
        partner = list(range(count))
        for i in range(first, count - 1, 2):
            partner[i], partner[i + 1] = i + 1, i
        return [(i, partner[i]) for i in range(count)]

    return pairs(0), pairs(1)


def edges_kernel(state_ref, zonal_ref, merid_ref, e_ref, o_ref):
    members, rows, levels, lon = state_ref.shape
    odd = lax.rem(lax.axis_index("lat"), 2)
    for out_ref, low in ((e_ref, odd), (o_ref, 1 - odd)):
        first = (1 - low) * (rows - 2)
        edge = (1 - low) * (rows - 1)
        for m in range(members):
            out_ref[2 * m] = state_ref[m, first]
            out_ref[2 * m + 1] = state_ref[m, first + 1]
        out_ref[2 * members] = zonal_ref[edge]
        out_ref[2 * members + 1] = merid_ref[edge]


def edge_messages(state, zonal, meridional):
    members, rows, levels, lon = state.shape
    shape = jax.ShapeDtypeStruct((2 * members + 2, levels, lon), jnp.float32)
    return pl.pallas_call(
        edges_kernel,
        out_shape=(shape, shape),
        in_specs=whole(3),
        out_specs=tuple(whole(2)),
        compiler_params=SMALL,
        name="edges",
    )(state, zonal, meridional)


def advance(south, middle, north, zonal, meridional):
    lon = middle.shape[-1]
    axis = middle.ndim - 1
    east = pltpu.roll(middle, lon - 1, axis)
    west = pltpu.roll(middle, 1, axis)
    return middle - step_size * (
        (zonal + middle) * (east - west) * 0.5 + meridional * (north - south) * 0.5
    )


def forecast_kernel(
    bands, state_ref, e_ref, o_ref, zonal_ref, merid_ref, dsum_ref, vsum_ref, out_ref
):
    members, rows, levels, lon = state_ref.shape
    band = lax.axis_index("lat")
    even = lax.rem(band, 2) == 0
    has_low = band > 0
    has_high = band < bands - 1

    def halo(i):
        e, o = e_ref[i], o_ref[i]
        low = jnp.where(has_low, jnp.where(even, o, e), 0.0)
        high = jnp.where(has_high, jnp.where(even, e, o), 0.0)
        return low, high

    z_low, z_high = halo(members * 2)
    m_low, m_high = halo(members * 2 + 1)
    zonal = [z_low] + [zonal_ref[r] for r in range(rows)] + [z_high]
    merid = [m_low] + [merid_ref[r] for r in range(rows)] + [m_high]
    for m in range(members):
        low0, high0 = halo(2 * m)
        low1, high1 = halo(2 * m + 1)
        q = [low0, low1] + [state_ref[m, r] for r in range(rows)] + [high0, high1]
        first = [
            advance(q[r], q[r + 1], q[r + 2], zonal[r], merid[r]) for r in range(rows + 2)
        ]
        for r in range(rows):
            out_ref[r, m] = advance(
                first[r], first[r + 1], first[r + 2], zonal[r + 1], merid[r + 1]
            )


def forecast(bands, state, e_msg, o_msg, zonal, merid, dsum, vsum):
    members, rows, levels, lon = state.shape
    size = state.size
    return pl.pallas_call(
        functools.partial(forecast_kernel, bands),
        out_shape=jax.ShapeDtypeStruct((rows, members, levels, lon), jnp.float32),
        in_specs=whole(5) + [pl.BlockSpec(memory_space=pl.ANY)] * 2,
        out_specs=pl.BlockSpec(memory_space=VM),
        cost_estimate=pl.CostEstimate(
            flops=24 * size, bytes_accessed=8 * size, transcendentals=0
        ),
        compiler_params=SMALL,
        name="forecast",
    )(state, e_msg, o_msg, zonal, merid, dsum, vsum)


def cells_kernel(cell_ref, value_ref, weight_ref, dsum_ref, vsum_ref):
    groups, regions, obs = cell_ref.shape
    lon = dsum_ref.shape[1]
    mine = lax.axis_index("member")
    weight = weight_ref[mine]
    cell_t = cell_ref[mine].T
    weight_t = weight.T
    value_t = (weight * value_ref[mine]).T
    index = lax.broadcasted_iota(jnp.int32, (obs, lon), 1)
    for r in range(regions):
        hit = jnp.broadcast_to(cell_t[:, r : r + 1], (obs, lon)) == index
        w = jnp.broadcast_to(weight_t[:, r : r + 1], (obs, lon))
        v = jnp.broadcast_to(value_t[:, r : r + 1], (obs, lon))
        dsum_ref[r : r + 1, :] = jnp.sum(jnp.where(hit, w, 0.0), axis=0, keepdims=True)
        vsum_ref[r : r + 1, :] = jnp.sum(jnp.where(hit, v, 0.0), axis=0, keepdims=True)


def per_cell(cells, values, weights, lon):
    groups, regions, obs = cells.shape
    shape = jax.ShapeDtypeStruct((regions, lon), jnp.float32)
    return pl.pallas_call(
        cells_kernel,
        out_shape=(shape, shape),
        in_specs=whole(3),
        out_specs=tuple(whole(2)),
        cost_estimate=pl.CostEstimate(
            flops=4 * regions * obs * lon,
            bytes_accessed=4 * (3 * regions * obs + 2 * regions * lon),
            transcendentals=0,
        ),
        compiler_params=SMALL,
        name="per_cell",
    )(cells, values, weights)


def split(x):
    high = x.astype(jnp.bfloat16)
    low = (x - high.astype(jnp.float32)).astype(jnp.bfloat16)
    return high, low


def product(a, b, dims=((1,), (0,))):
    def dot(x, y):
        return lax.dot_general(x, y, (dims, ((), ())), preferred_element_type=jnp.float32)

    return dot(a[0], b[0]) + (dot(a[0], b[1]) + dot(a[1], b[0]))


def analysis_kernel(regions, ens_ref, dsum_ref, vsum_ref, out_ref):
    size, lon = ens_ref.shape
    count = size // regions

    def over_members(x):
        if regions == 1:
            return jnp.sum(x, axis=0, keepdims=True)
        return jnp.sum(x.reshape(count, regions, x.shape[-1]), axis=0)

    def spread(x):
        if regions == 1:
            return jnp.broadcast_to(x, (size, x.shape[-1]))
        x = jnp.broadcast_to(x[None], (count, regions, x.shape[-1]))
        return x.reshape(size, x.shape[-1])

    ens = ens_ref[...]
    dsum = dsum_ref[...]
    mean = over_members(ens) * (1.0 / count)
    pert = ens - spread(mean)
    pull = vsum_ref[...] - dsum * mean

    row = lax.broadcasted_iota(jnp.int32, (size, size), 0)
    col = lax.broadcasted_iota(jnp.int32, (size, size), 1)
    same = lax.rem(row, regions) == lax.rem(col, regions)
    one = jnp.where(row == col, 1.0, 0.0)

    pert_s = split(pert)
    gram = product(split(pert * spread(dsum)), pert_s, ((1,), (1,)))
    system = jnp.where(same, gram, 0.0) + (count - 1.0) * one
    total = over_members(jnp.sum(system * system, axis=1, keepdims=True))
    frob = jnp.sqrt(total)
    iterate = system * spread(1.0 / frob)
    iterate_s = split(iterate)
    inverse_s = None
    for sweep in range(SWEEPS):
        step = iterate if inverse_s is None else product(inverse_s, iterate_s)
        factor_s = split(1.5 * one - 0.5 * step)
        if sweep == SWEEPS - 1:
            break
        iterate_s = split(product(iterate_s, factor_s))
        inverse_s = factor_s if inverse_s is None else split(product(factor_s, inverse_s))
    part_s = split(product(inverse_s, pert_s))
    update = product(factor_s, part_s) * spread(lax.rsqrt(frob))
    gain = jnp.sum(update * spread(pull), axis=1, keepdims=True)
    shift = mean + over_members(update * gain)
    out_ref[...] = spread(shift) + jnp.sqrt(count - 1.0) * update


def analysis(ens, dsum, vsum):
    size, lon = ens.shape
    regions = dsum.shape[0]
    return pl.pallas_call(
        functools.partial(analysis_kernel, regions),
        out_shape=jax.ShapeDtypeStruct((size, lon), jnp.float32),
        in_specs=whole(3),
        out_specs=pl.BlockSpec(memory_space=VM),
        cost_estimate=pl.CostEstimate(
            flops=48 * size * size * lon, bytes_accessed=8 * size * lon, transcendentals=0
        ),
        compiler_params=SMALL,
        name="analysis",
    )(ens, dsum, vsum)


def body(state, zonal_wind, meridional_wind, obs_cell, obs_value, obs_weight):
    members_dev, lat_dev, levels, longitudes = state.shape
    groups = lax.axis_size("member")
    bands = lax.axis_size("lat")
    regions = lat_dev * levels // groups
    count = members_dev * groups

    first_round, second_round = pair_rounds(bands)
    e_msg, o_msg = edge_messages(state, zonal_wind, meridional_wind)
    e_msg = lax.ppermute(e_msg, "lat", first_round)
    o_msg = lax.ppermute(o_msg, "lat", second_round)

    def grouped(x):
        return x.reshape(groups, regions, x.shape[-1])

    dsum, vsum = per_cell(
        grouped(obs_cell), grouped(obs_value), grouped(obs_weight), longitudes
    )
    field = forecast(
        bands, state, e_msg, o_msg, zonal_wind, meridional_wind, dsum, vsum
    )
    blocks = field.transpose(1, 0, 2, 3).reshape(members_dev, groups, regions, longitudes)
    ensemble = lax.all_to_all(
        blocks.transpose(1, 0, 2, 3), "member", split_axis=0, concat_axis=0, tiled=True
    )
    analysed = analysis(ensemble.reshape(count * regions, longitudes), dsum, vsum)
    returned = lax.all_to_all(
        analysed.reshape(groups, members_dev, regions, longitudes),
        "member",
        split_axis=0,
        concat_axis=0,
        tiled=True,
    )
    return returned.transpose(1, 0, 2, 3).reshape(state.shape)


def solution(mesh):
    in_specs = (
        P("member", "lat", None, None),
        P("lat", None, None),
        P("lat", None, None),
        P("lat", None, None),
        P("lat", None, None),
        P("lat", None, None),
    )
    out_specs = P("member", "lat", None, None)
    return jax.shard_map(body, mesh=mesh, in_specs=in_specs, out_specs=out_specs, check_vma=False)
```

```python
import functools

import jax
import jax.numpy as jnp
from jax import lax
from jax.experimental import pallas as pl
from jax.experimental.pallas import tpu as pltpu
from jax.sharding import PartitionSpec as P

SWEEPS = 3
step_size = 0.3
VM = pltpu.VMEM
SMALL = pltpu.CompilerParams(vmem_limit_bytes=12 * 2**20)


def whole(n):
    return [pl.BlockSpec(memory_space=VM)] * n


def pair_rounds(count):
    def pairs(first):
        partner = list(range(count))
        for i in range(first, count - 1, 2):
            partner[i], partner[i + 1] = i + 1, i
        return [(i, partner[i]) for i in range(count)]

    return pairs(0), pairs(1)


def edges_kernel(state_ref, zonal_ref, merid_ref, e_ref, o_ref, sems):
    members, rows, levels, lon = state_ref.shape
    odd = lax.rem(lax.axis_index("lat"), 2)
    copies = []
    for out_ref, low in ((e_ref, odd), (o_ref, 1 - odd)):
        first = (1 - low) * (rows - 2)
        edge = (1 - low) * (rows - 1)
        parts = [
            (state_ref.at[m, pl.ds(first, 2)], out_ref.at[pl.ds(2 * m, 2)])
            for m in range(members)
        ]
        parts.append((zonal_ref.at[edge], out_ref.at[2 * members]))
        parts.append((merid_ref.at[edge], out_ref.at[2 * members + 1]))
        for source, target in parts:
            copies.append(pltpu.make_async_copy(source, target, sems.at[len(copies)]))
    for copy in copies:
        copy.start()
    for copy in copies:
        copy.wait()


def edge_messages(state, zonal, meridional):
    members, rows, levels, lon = state.shape
    shape = jax.ShapeDtypeStruct((2 * members + 2, levels, lon), jnp.float32)
    held = [
        pltpu.with_memory_space_constraint(x, pltpu.HBM)
        for x in (state, zonal, meridional)
    ]
    return pl.pallas_call(
        edges_kernel,
        out_shape=(shape, shape),
        in_specs=[pl.BlockSpec(memory_space=pltpu.HBM)] * 3,
        out_specs=tuple(whole(2)),
        scratch_shapes=[pltpu.SemaphoreType.DMA((2 * members + 4,))],
        compiler_params=SMALL,
        name="edges",
    )(*held)


def advance(south, middle, north, zonal, meridional):
    lon = middle.shape[-1]
    axis = middle.ndim - 1
    east = pltpu.roll(middle, lon - 1, axis)
    west = pltpu.roll(middle, 1, axis)
    return middle - step_size * (
        (zonal + middle) * (east - west) * 0.5 + meridional * (north - south) * 0.5
    )


def forecast_kernel(
    bands, state_ref, e_ref, o_ref, zonal_ref, merid_ref, dsum_ref, vsum_ref, out_ref
):
    members, rows, levels, lon = state_ref.shape
    band = lax.axis_index("lat")
    even = lax.rem(band, 2) == 0
    has_low = band > 0
    has_high = band < bands - 1

    def halo(i):
        e, o = e_ref[i], o_ref[i]
        low = jnp.where(has_low, jnp.where(even, o, e), 0.0)
        high = jnp.where(has_high, jnp.where(even, e, o), 0.0)
        return low, high

    z_low, z_high = halo(members * 2)
    m_low, m_high = halo(members * 2 + 1)
    zonal = [z_low] + [zonal_ref[r] for r in range(rows)] + [z_high]
    merid = [m_low] + [merid_ref[r] for r in range(rows)] + [m_high]
    for m in range(members):
        low0, high0 = halo(2 * m)
        low1, high1 = halo(2 * m + 1)
        q = [low0, low1] + [state_ref[m, r] for r in range(rows)] + [high0, high1]
        first = [
            advance(q[r], q[r + 1], q[r + 2], zonal[r], merid[r]) for r in range(rows + 2)
        ]
        for r in range(rows):
            out_ref[r, m] = advance(
                first[r], first[r + 1], first[r + 2], zonal[r + 1], merid[r + 1]
            )


def forecast(bands, state, e_msg, o_msg, zonal, merid, dsum, vsum):
    members, rows, levels, lon = state.shape
    size = state.size
    return pl.pallas_call(
        functools.partial(forecast_kernel, bands),
        out_shape=jax.ShapeDtypeStruct((rows, members, levels, lon), jnp.float32),
        in_specs=whole(5) + [pl.BlockSpec(memory_space=pl.ANY)] * 2,
        out_specs=pl.BlockSpec(memory_space=VM),
        cost_estimate=pl.CostEstimate(
            flops=24 * size, bytes_accessed=8 * size, transcendentals=0
        ),
        compiler_params=SMALL,
        name="forecast",
    )(state, e_msg, o_msg, zonal, merid, dsum, vsum)


def cells_kernel(cell_ref, value_ref, weight_ref, dsum_ref, vsum_ref):
    groups, regions, obs = cell_ref.shape
    lon = dsum_ref.shape[1]
    mine = lax.axis_index("member")
    weight = weight_ref[mine]
    cell_t = cell_ref[mine].T
    weight_t = weight.T
    value_t = (weight * value_ref[mine]).T
    index = lax.broadcasted_iota(jnp.int32, (obs, lon), 1)
    for r in range(regions):
        hit = jnp.broadcast_to(cell_t[:, r : r + 1], (obs, lon)) == index
        w = jnp.broadcast_to(weight_t[:, r : r + 1], (obs, lon))
        v = jnp.broadcast_to(value_t[:, r : r + 1], (obs, lon))
        dsum_ref[r : r + 1, :] = jnp.sum(jnp.where(hit, w, 0.0), axis=0, keepdims=True)
        vsum_ref[r : r + 1, :] = jnp.sum(jnp.where(hit, v, 0.0), axis=0, keepdims=True)


def per_cell(cells, values, weights, lon):
    groups, regions, obs = cells.shape
    shape = jax.ShapeDtypeStruct((regions, lon), jnp.float32)
    return pl.pallas_call(
        cells_kernel,
        out_shape=(shape, shape),
        in_specs=whole(3),
        out_specs=tuple(whole(2)),
        cost_estimate=pl.CostEstimate(
            flops=4 * regions * obs * lon,
            bytes_accessed=4 * (3 * regions * obs + 2 * regions * lon),
            transcendentals=0,
        ),
        compiler_params=SMALL,
        name="per_cell",
    )(cells, values, weights)


def split(x):
    high = x.astype(jnp.bfloat16)
    low = (x - high.astype(jnp.float32)).astype(jnp.bfloat16)
    return high, low


def product(a, b, dims=((1,), (0,))):
    def dot(x, y):
        return lax.dot_general(x, y, (dims, ((), ())), preferred_element_type=jnp.float32)

    return dot(a[0], b[0]) + (dot(a[0], b[1]) + dot(a[1], b[0]))


def analysis_kernel(regions, ens_ref, dsum_ref, vsum_ref, out_ref):
    size, lon = ens_ref.shape
    count = size // regions

    def over_members(x):
        if regions == 1:
            return jnp.sum(x, axis=0, keepdims=True)
        return jnp.sum(x.reshape(count, regions, x.shape[-1]), axis=0)

    def spread(x):
        if regions == 1:
            return jnp.broadcast_to(x, (size, x.shape[-1]))
        x = jnp.broadcast_to(x[None], (count, regions, x.shape[-1]))
        return x.reshape(size, x.shape[-1])

    ens = ens_ref[...]
    dsum = dsum_ref[...]
    mean = over_members(ens) * (1.0 / count)
    pert = ens - spread(mean)
    pull = vsum_ref[...] - dsum * mean

    row = lax.broadcasted_iota(jnp.int32, (size, size), 0)
    col = lax.broadcasted_iota(jnp.int32, (size, size), 1)
    same = lax.rem(row, regions) == lax.rem(col, regions)
    one = jnp.where(row == col, 1.0, 0.0)

    pert_s = split(pert)
    gram = product(split(pert * spread(dsum)), pert_s, ((1,), (1,)))
    system = jnp.where(same, gram, 0.0) + (count - 1.0) * one
    total = over_members(jnp.sum(system * system, axis=1, keepdims=True))
    frob = jnp.sqrt(total)
    iterate = system * spread(1.0 / frob)
    iterate_s = split(iterate)
    inverse_s = None
    for sweep in range(SWEEPS):
        step = iterate if inverse_s is None else product(inverse_s, iterate_s)
        factor_s = split(1.5 * one - 0.5 * step)
        if sweep == SWEEPS - 1:
            break
        iterate_s = split(product(iterate_s, factor_s))
        inverse_s = factor_s if inverse_s is None else split(product(factor_s, inverse_s))
    part_s = split(product(inverse_s, pert_s))
    update = product(factor_s, part_s) * spread(lax.rsqrt(frob))
    gain = jnp.sum(update * spread(pull), axis=1, keepdims=True)
    shift = mean + over_members(update * gain)
    out_ref[...] = spread(shift) + jnp.sqrt(count - 1.0) * update


def analysis(ens, dsum, vsum):
    size, lon = ens.shape
    regions = dsum.shape[0]
    return pl.pallas_call(
        functools.partial(analysis_kernel, regions),
        out_shape=jax.ShapeDtypeStruct((size, lon), jnp.float32),
        in_specs=whole(3),
        out_specs=pl.BlockSpec(memory_space=VM),
        cost_estimate=pl.CostEstimate(
            flops=48 * size * size * lon, bytes_accessed=8 * size * lon, transcendentals=0
        ),
        compiler_params=SMALL,
        name="analysis",
    )(ens, dsum, vsum)


def body(state, zonal_wind, meridional_wind, obs_cell, obs_value, obs_weight):
    members_dev, lat_dev, levels, longitudes = state.shape
    groups = lax.axis_size("member")
    bands = lax.axis_size("lat")
    regions = lat_dev * levels // groups
    count = members_dev * groups

    first_round, second_round = pair_rounds(bands)
    e_msg, o_msg = edge_messages(state, zonal_wind, meridional_wind)
    e_msg = lax.ppermute(e_msg, "lat", first_round)
    o_msg = lax.ppermute(o_msg, "lat", second_round)

    def grouped(x):
        return x.reshape(groups, regions, x.shape[-1])

    dsum, vsum = per_cell(
        grouped(obs_cell), grouped(obs_value), grouped(obs_weight), longitudes
    )
    field = forecast(
        bands, state, e_msg, o_msg, zonal_wind, meridional_wind, dsum, vsum
    )
    blocks = field.transpose(1, 0, 2, 3).reshape(members_dev, groups, regions, longitudes)
    ensemble = lax.all_to_all(
        blocks.transpose(1, 0, 2, 3), "member", split_axis=0, concat_axis=0, tiled=True
    )
    analysed = analysis(ensemble.reshape(count * regions, longitudes), dsum, vsum)
    returned = lax.all_to_all(
        analysed.reshape(groups, members_dev, regions, longitudes),
        "member",
        split_axis=0,
        concat_axis=0,
        tiled=True,
    )
    return returned.transpose(1, 0, 2, 3).reshape(state.shape)


def solution(mesh):
    in_specs = (
        P("member", "lat", None, None),
        P("lat", None, None),
        P("lat", None, None),
        P("lat", None, None),
        P("lat", None, None),
        P("lat", None, None),
    )
    out_specs = P("member", "lat", None, None)
    return jax.shard_map(body, mesh=mesh, in_specs=in_specs, out_specs=out_specs, check_vma=False)
```

```python
import functools

import jax
import jax.numpy as jnp
from jax import lax
from jax.experimental import pallas as pl
from jax.experimental.pallas import tpu as pltpu
from jax.sharding import PartitionSpec as P

SWEEPS = 3
step_size = 0.3
VM = pltpu.VMEM
SMALL = pltpu.CompilerParams(vmem_limit_bytes=12 * 2**20)


def whole(n):
    return [pl.BlockSpec(memory_space=VM)] * n


def place(bands):
    member, band = lax.axis_index("member"), lax.axis_index("lat")
    core, chip = lax.rem(member, 2), lax.div(member, 2)
    high = lax.rem(core + band, 2) == 0
    at_edge = jnp.where(high, band == bands - 1, band == 0)
    return chip, high, at_edge


def halo_pairs(groups, bands):
    pairs = []
    for member in range(groups):
        for band in range(bands):
            step = 1 if (member + band) % 2 == 0 else -1
            other = band + step if 0 <= band + step < bands else band
            pairs.append((member * bands + band, member * bands + other))
    return pairs


def swap(x, groups, distance):
    return lax.ppermute(x, "member", [(i, i ^ distance) for i in range(groups)])


def stage_kernel(bands, *refs):
    sources, targets, sems = refs[:6], refs[6:12], refs[12]
    chip, high, at_edge = place(bands)
    mine = jnp.where(high, sources[3].shape[0] // 2, 0) + chip
    sources = list(sources[:3]) + [ref.at[mine] for ref in sources[3:]]
    copies = [
        pltpu.make_async_copy(source, target, sems.at[i])
        for i, (source, target) in enumerate(zip(sources, targets))
    ]
    for copy in copies:
        copy.start()
    for copy in copies:
        copy.wait()


def stage(bands, fields, tables):
    shapes = [x.shape for x in fields] + [x.shape[1:] for x in tables]
    args = [pltpu.with_memory_space_constraint(x, pltpu.HBM) for x in (*fields, *tables)]
    return pl.pallas_call(
        functools.partial(stage_kernel, bands),
        out_shape=tuple(jax.ShapeDtypeStruct(n, x.dtype) for n, x in zip(shapes, args)),
        in_specs=[pl.BlockSpec(memory_space=pltpu.HBM)] * 6,
        out_specs=tuple(whole(6)),
        scratch_shapes=[pltpu.SemaphoreType.DMA((6,))],
        cost_estimate=pl.CostEstimate(flops=0, bytes_accessed=2**21, transcendentals=0),
        compiler_params=SMALL,
        name="stage",
    )(*args)


def edges_kernel(bands, own_ref, partner_ref, zonal_ref, merid_ref, out_ref):
    members, rows, levels, lon = own_ref.shape
    chip, high, at_edge = place(bands)
    first = jnp.where(high, rows - 2, 0)
    edge = jnp.where(high, rows - 1, 0)
    for m in range(2 * members):
        ref = own_ref if m < members else partner_ref
        out_ref[2 * m] = ref[m % members, first]
        out_ref[2 * m + 1] = ref[m % members, first + 1]
    out_ref[4 * members] = zonal_ref[edge]
    out_ref[4 * members + 1] = merid_ref[edge]


def edge_message(bands, own, partner, zonal, merid):
    members, rows, levels, lon = own.shape
    return pl.pallas_call(
        functools.partial(edges_kernel, bands),
        out_shape=jax.ShapeDtypeStruct((4 * members + 2, levels, lon), jnp.float32),
        in_specs=whole(4),
        out_specs=pl.BlockSpec(memory_space=VM),
        compiler_params=SMALL,
        name="edges",
    )(own, partner, zonal, merid)


def advance(south, middle, north, zonal, meridional):
    lon = middle.shape[-1]
    axis = middle.ndim - 1
    east = pltpu.roll(middle, lon - 1, axis)
    west = pltpu.roll(middle, 1, axis)
    return middle - step_size * (
        (zonal + middle) * (east - west) * 0.5 + meridional * (north - south) * 0.5
    )


def forecast_kernel(
    bands,
    crossed,
    own_ref,
    partner_ref,
    halo_ref,
    zonal_ref,
    merid_ref,
    dsum_ref,
    vsum_ref,
    *refs,
):
    out_refs, first_ref = refs[:-1], refs[-1]
    members, rows, levels, lon = own_ref.shape
    half = rows // 2
    chip, high, at_edge = place(bands)
    base = jnp.where(high, half, 0)

    def halo(i):
        return jnp.where(at_edge, 0.0, halo_ref[i])

    def winds(ref, outside):
        inside = [ref[base + r] for r in range(half)]
        before = jnp.where(high, ref[half - 1], outside)
        after = jnp.where(high, outside, ref[half])
        return [before, *inside, after]

    zonal = winds(zonal_ref, halo(4 * members))
    merid = winds(merid_ref, halo(4 * members + 1))
    for m in range(2 * members):
        ref, k = (own_ref if m < members else partner_ref), m % members
        outside = [halo(2 * m), halo(2 * m + 1)]
        q = [jnp.where(high, ref[k, half - 2 + i], outside[i]) for i in range(2)]
        q += [ref[k, base + r] for r in range(half)]
        q += [jnp.where(high, outside[i], ref[k, half + i]) for i in range(2)]
        for r in range(half + 2):
            first_ref[r, m] = advance(q[r], q[r + 1], q[r + 2], zonal[r], merid[r])
    for t in range(half):
        r = row_of(chip, t, crossed)
        zonal_row, merid_row = zonal_ref[base + r], merid_ref[base + r]
        for m in range(2 * members):
            out_refs[t][m] = advance(
                first_ref[r, m], first_ref[r + 1, m], first_ref[r + 2, m], zonal_row, merid_row
            )


def row_of(chip, t, crossed):
    return lax.bitwise_xor(chip, t) if crossed else t


def forecast(bands, crossed, own, partner, halo, zonal, merid, dsum, vsum):
    members, rows, levels, lon = own.shape
    half = rows // 2
    size = own.size
    shape = jax.ShapeDtypeStruct((2 * members, levels, lon), jnp.float32)
    return pl.pallas_call(
        functools.partial(forecast_kernel, bands, crossed),
        out_shape=(shape,) * half,
        in_specs=whole(5) + [pl.BlockSpec(memory_space=pl.ANY)] * 2,
        out_specs=tuple(whole(half)),
        scratch_shapes=[VM((half + 2, 2 * members, levels, lon), jnp.float32)],
        cost_estimate=pl.CostEstimate(
            flops=24 * size, bytes_accessed=8 * size, transcendentals=0
        ),
        compiler_params=SMALL,
        name="forecast",
    )(own, partner, halo, zonal, merid, dsum, vsum)


def cells_kernel(cell_ref, value_ref, weight_ref, dsum_ref, vsum_ref):
    regions, obs = cell_ref.shape
    lon = dsum_ref.shape[1]
    weight = weight_ref[...]
    cell_t = cell_ref[...].T
    weight_t = weight.T
    value_t = (weight * value_ref[...]).T
    index = lax.broadcasted_iota(jnp.int32, (obs, lon), 1)
    for r in range(regions):
        hit = jnp.broadcast_to(cell_t[:, r : r + 1], (obs, lon)) == index
        w = jnp.broadcast_to(weight_t[:, r : r + 1], (obs, lon))
        v = jnp.broadcast_to(value_t[:, r : r + 1], (obs, lon))
        dsum_ref[r : r + 1, :] = jnp.sum(jnp.where(hit, w, 0.0), axis=0, keepdims=True)
        vsum_ref[r : r + 1, :] = jnp.sum(jnp.where(hit, v, 0.0), axis=0, keepdims=True)


def per_cell(cells, values, weights, lon):
    regions, obs = cells.shape
    shape = jax.ShapeDtypeStruct((regions, lon), jnp.float32)
    return pl.pallas_call(
        cells_kernel,
        out_shape=(shape, shape),
        in_specs=whole(3),
        out_specs=tuple(whole(2)),
        cost_estimate=pl.CostEstimate(
            flops=4 * regions * obs * lon,
            bytes_accessed=4 * (3 * regions * obs + 2 * regions * lon),
            transcendentals=0,
        ),
        compiler_params=SMALL,
        name="per_cell",
    )(cells, values, weights)


def split(x):
    high = x.astype(jnp.bfloat16)
    low = (x - high.astype(jnp.float32)).astype(jnp.bfloat16)
    return high, low


def product(a, b, dims=((1,), (0,))):
    def dot(x, y):
        return lax.dot_general(x, y, (dims, ((), ())), preferred_element_type=jnp.float32)

    return dot(a[0], b[0]) + (dot(a[0], b[1]) + dot(a[1], b[0]))


def analysis_kernel(regions, parts, *refs):
    ens_refs, (dsum_ref, vsum_ref) = refs[:parts], refs[parts : parts + 2]
    out_refs = refs[parts + 2 :]
    share, lon = ens_refs[0].shape
    size = share * parts
    count = size // regions

    def over_members(x):
        if regions == 1:
            return jnp.sum(x, axis=0, keepdims=True)
        return jnp.sum(x.reshape(count, regions, x.shape[-1]), axis=0)

    def spread(x):
        if regions == 1:
            return jnp.broadcast_to(x, (size, x.shape[-1]))
        x = jnp.broadcast_to(x[None], (count, regions, x.shape[-1]))
        return x.reshape(size, x.shape[-1])

    ens = jnp.concatenate([ref[...] for ref in ens_refs], axis=0)
    dsum = dsum_ref[...]
    mean = over_members(ens) * (1.0 / count)
    pert = ens - spread(mean)
    pull = vsum_ref[...] - dsum * mean

    row = lax.broadcasted_iota(jnp.int32, (size, size), 0)
    col = lax.broadcasted_iota(jnp.int32, (size, size), 1)
    same = lax.rem(row, regions) == lax.rem(col, regions)
    one = jnp.where(row == col, 1.0, 0.0)

    pert_s = split(pert)
    gram = product(split(pert * spread(dsum)), pert_s, ((1,), (1,)))
    system = jnp.where(same, gram, 0.0) + (count - 1.0) * one
    total = over_members(jnp.sum(system * system, axis=1, keepdims=True))
    frob = jnp.sqrt(total)
    iterate = system * spread(1.0 / frob)
    iterate_s = split(iterate)
    inverse_s = None
    for sweep in range(SWEEPS):
        step = iterate if inverse_s is None else product(inverse_s, iterate_s)
        factor_s = split(1.5 * one - 0.5 * step)
        if sweep == SWEEPS - 1:
            break
        iterate_s = split(product(iterate_s, factor_s))
        inverse_s = factor_s if inverse_s is None else split(product(factor_s, inverse_s))
    part_s = split(product(inverse_s, pert_s))
    update = product(factor_s, part_s) * spread(lax.rsqrt(frob))
    gain = jnp.sum(update * spread(pull), axis=1, keepdims=True)
    shift = mean + over_members(update * gain)
    result = spread(shift) + jnp.sqrt(count - 1.0) * update
    for i, ref in enumerate(out_refs):
        ref[...] = result[i * share : (i + 1) * share]


def analysis(ens, dsum, vsum):
    parts = len(ens)
    share, lon = ens[0].shape
    size = share * parts
    regions = dsum.shape[0]
    return pl.pallas_call(
        functools.partial(analysis_kernel, regions, parts),
        out_shape=(jax.ShapeDtypeStruct((share, lon), jnp.float32),) * parts,
        in_specs=whole(parts + 2),
        out_specs=tuple(whole(parts)),
        cost_estimate=pl.CostEstimate(
            flops=48 * size * size * lon, bytes_accessed=8 * size * lon, transcendentals=0
        ),
        compiler_params=SMALL,
        name="analysis",
    )(*ens, dsum, vsum)


def place_rows_kernel(bands, crossed, got_ref, *refs):
    half_refs, out_ref, sems = refs[:-2], refs[-2], refs[-1]
    half = len(half_refs)
    members = out_ref.shape[0]
    chip, high, at_edge = place(bands)
    base = jnp.where(high, half, 0)
    copies = []
    for t, ref in enumerate(half_refs):
        r = row_of(chip, t, crossed)
        for source, row in ((ref.at[pl.ds(0, members)], base + r), (got_ref.at[t], half - base + r)):
            copies.append(
                pltpu.make_async_copy(source, out_ref.at[:, row], sems.at[len(copies)])
            )
    for copy in copies:
        copy.start()
    for copy in copies:
        copy.wait()


def place_rows(bands, crossed, got, halves, shape):
    half = len(halves)
    return pl.pallas_call(
        functools.partial(place_rows_kernel, bands, crossed),
        out_shape=jax.ShapeDtypeStruct(shape, jnp.float32),
        in_specs=whole(1 + half),
        out_specs=pl.BlockSpec(memory_space=pltpu.HBM),
        scratch_shapes=[pltpu.SemaphoreType.DMA((2 * half,))],
        compiler_params=SMALL,
        name="place_rows",
    )(got, *halves)


def body(state, zonal_wind, meridional_wind, obs_cell, obs_value, obs_weight):
    members, rows, levels, lon = state.shape
    groups = lax.axis_size("member")
    bands = lax.axis_size("lat")
    half = rows // 2
    chips = groups // 2
    regions = half * levels // chips
    crossed = chips == half and chips <= 4 and chips & (chips - 1) == 0

    def grouped(x):
        return x.reshape(groups, regions, x.shape[-1])

    partner = swap(state, groups, 1)
    own, zonal, merid, *tables = stage(
        bands,
        (state, zonal_wind, meridional_wind),
        (grouped(obs_cell), grouped(obs_value), grouped(obs_weight)),
    )
    message = edge_message(bands, own, partner, zonal, merid)
    halo = lax.ppermute(message, ("member", "lat"), halo_pairs(groups, bands))

    dsum, vsum = per_cell(*tables, lon)
    sent = forecast(bands, crossed, own, partner, halo, zonal, merid, dsum, vsum)
    same_core = [list(range(core, groups, 2)) for core in range(2)]

    def exchange(blocks):
        if crossed:
            return [blocks[0]] + [swap(b, groups, 2 * t) for t, b in enumerate(blocks) if t]
        return [
            lax.all_to_all(
                blocks[0], "member", 0, 0, tiled=True, axis_index_groups=same_core
            )
        ]

    if not crossed:
        field = jnp.stack(sent, axis=1).reshape(2 * members, chips, regions, lon)
        sent = [field.transpose(1, 0, 2, 3)]
    ensemble = exchange(sent)
    flat = [x.reshape(-1, lon) for x in ensemble]
    analysed = analysis(flat, dsum, vsum)
    back = exchange([x.reshape(e.shape) for x, e in zip(analysed, ensemble)])
    if not crossed:
        field = back[0].transpose(1, 0, 2, 3).reshape(2 * members, half, levels, lon)
        back = [field[:, t] for t in range(half)]
    got = swap(jnp.stack([b[members:] for b in back]), groups, 1)
    return place_rows(bands, crossed, got, back, state.shape)


def solution(mesh):
    in_specs = (
        P("member", "lat", None, None),
        P("lat", None, None),
        P("lat", None, None),
        P("lat", None, None),
        P("lat", None, None),
        P("lat", None, None),
    )
    out_specs = P("member", "lat", None, None)
    return jax.shard_map(body, mesh=mesh, in_specs=in_specs, out_specs=out_specs, check_vma=False)
```

```python
import functools

import jax
import jax.numpy as jnp
from jax import lax
from jax.experimental import pallas as pl
from jax.experimental.pallas import tpu as pltpu
from jax.sharding import PartitionSpec as P

SWEEPS = 3
step_size = 0.3
VM = pltpu.VMEM
SMALL = pltpu.CompilerParams(vmem_limit_bytes=12 * 2**20)


def whole(n):
    return [pl.BlockSpec(memory_space=VM)] * n


def place(bands):
    member, band = lax.axis_index("member"), lax.axis_index("lat")
    core, chip = lax.rem(member, 2), lax.div(member, 2)
    high = lax.rem(core + band, 2) == 0
    at_edge = jnp.where(high, band == bands - 1, band == 0)
    return chip, high, at_edge


def halo_pairs(groups, bands):
    pairs = []
    for member in range(groups):
        for band in range(bands):
            other, peer = band + (1 if (member + band) % 2 == 0 else -1), member
            if not 0 <= other < bands:
                other, peer = band, member ^ 2 if groups % 4 == 0 else member
            pairs.append((member * bands + band, peer * bands + other))
    return pairs


def swap(x, groups, distance):
    return lax.ppermute(x, "member", [(i, i ^ distance) for i in range(groups)])


def stage_kernel(bands, *refs):
    sources, targets, sems = refs[:6], refs[6:12], refs[12]
    chip, high, at_edge = place(bands)
    mine = jnp.where(high, sources[3].shape[0] // 2, 0) + chip
    sources = list(sources[:3]) + [ref.at[mine] for ref in sources[3:]]
    copies = [
        pltpu.make_async_copy(source, target, sems.at[i])
        for i, (source, target) in enumerate(zip(sources, targets))
    ]
    for copy in copies:
        copy.start()
    for copy in copies:
        copy.wait()


def stage(bands, fields, tables):
    shapes = [x.shape for x in fields] + [x.shape[1:] for x in tables]
    args = [pltpu.with_memory_space_constraint(x, pltpu.HBM) for x in (*fields, *tables)]
    return pl.pallas_call(
        functools.partial(stage_kernel, bands),
        out_shape=tuple(jax.ShapeDtypeStruct(n, x.dtype) for n, x in zip(shapes, args)),
        in_specs=[pl.BlockSpec(memory_space=pltpu.HBM)] * 6,
        out_specs=tuple(whole(6)),
        scratch_shapes=[pltpu.SemaphoreType.DMA((6,))],
        cost_estimate=pl.CostEstimate(flops=0, bytes_accessed=2**21, transcendentals=0),
        compiler_params=SMALL,
        name="stage",
    )(*args)


def edges_kernel(bands, own_ref, partner_ref, zonal_ref, merid_ref, out_ref):
    members, rows, levels, lon = own_ref.shape
    chip, high, at_edge = place(bands)
    first = jnp.where(high, rows - 2, 0)
    edge = jnp.where(high, rows - 1, 0)
    for m in range(2 * members):
        ref = own_ref if m < members else partner_ref
        out_ref[2 * m] = ref[m % members, first]
        out_ref[2 * m + 1] = ref[m % members, first + 1]
    out_ref[4 * members] = zonal_ref[edge]
    out_ref[4 * members + 1] = merid_ref[edge]


def edge_message(bands, own, partner, zonal, merid):
    members, rows, levels, lon = own.shape
    return pl.pallas_call(
        functools.partial(edges_kernel, bands),
        out_shape=jax.ShapeDtypeStruct((4 * members + 2, levels, lon), jnp.float32),
        in_specs=whole(4),
        out_specs=pl.BlockSpec(memory_space=VM),
        compiler_params=SMALL,
        name="edges",
    )(own, partner, zonal, merid)


def advance(south, middle, north, zonal, meridional):
    lon = middle.shape[-1]
    axis = middle.ndim - 1
    east = pltpu.roll(middle, lon - 1, axis)
    west = pltpu.roll(middle, 1, axis)
    return middle - step_size * (
        (zonal + middle) * (east - west) * 0.5 + meridional * (north - south) * 0.5
    )


def forecast_kernel(
    bands,
    crossed,
    own_ref,
    partner_ref,
    halo_ref,
    zonal_ref,
    merid_ref,
    dsum_ref,
    vsum_ref,
    *refs,
):
    out_refs, first_ref = refs[:-1], refs[-1]
    members, rows, levels, lon = own_ref.shape
    half = rows // 2
    chip, high, at_edge = place(bands)
    base = jnp.where(high, half, 0)

    def halo(i):
        return jnp.where(at_edge, 0.0, halo_ref[i])

    def winds(ref, outside):
        inside = [ref[base + r] for r in range(half)]
        before = jnp.where(high, ref[half - 1], outside)
        after = jnp.where(high, outside, ref[half])
        return [before, *inside, after]

    zonal = winds(zonal_ref, halo(4 * members))
    merid = winds(merid_ref, halo(4 * members + 1))
    for m in range(2 * members):
        ref, k = (own_ref if m < members else partner_ref), m % members
        outside = [halo(2 * m), halo(2 * m + 1)]
        q = [jnp.where(high, ref[k, half - 2 + i], outside[i]) for i in range(2)]
        q += [ref[k, base + r] for r in range(half)]
        q += [jnp.where(high, outside[i], ref[k, half + i]) for i in range(2)]
        for r in range(half + 2):
            first_ref[r, m] = advance(q[r], q[r + 1], q[r + 2], zonal[r], merid[r])
    for t in range(half):
        r = row_of(chip, t, crossed)
        zonal_row, merid_row = zonal_ref[base + r], merid_ref[base + r]
        for m in range(2 * members):
            out_refs[t][m] = advance(
                first_ref[r, m], first_ref[r + 1, m], first_ref[r + 2, m], zonal_row, merid_row
            )


def row_of(chip, t, crossed):
    return lax.bitwise_xor(chip, t) if crossed else t


def forecast(bands, crossed, own, partner, halo, zonal, merid, dsum, vsum):
    members, rows, levels, lon = own.shape
    half = rows // 2
    size = own.size
    shape = jax.ShapeDtypeStruct((2 * members, levels, lon), jnp.float32)
    return pl.pallas_call(
        functools.partial(forecast_kernel, bands, crossed),
        out_shape=(shape,) * half,
        in_specs=whole(5) + [pl.BlockSpec(memory_space=pl.ANY)] * 2,
        out_specs=tuple(whole(half)),
        scratch_shapes=[VM((half + 2, 2 * members, levels, lon), jnp.float32)],
        cost_estimate=pl.CostEstimate(
            flops=24 * size, bytes_accessed=8 * size, transcendentals=0
        ),
        compiler_params=SMALL,
        name="forecast",
    )(own, partner, halo, zonal, merid, dsum, vsum)


def cells_kernel(cell_ref, value_ref, weight_ref, dsum_ref, vsum_ref):
    regions, obs = cell_ref.shape
    lon = dsum_ref.shape[1]
    weight = weight_ref[...]
    cell_t = cell_ref[...].T
    weight_t = weight.T
    value_t = (weight * value_ref[...]).T
    index = lax.broadcasted_iota(jnp.int32, (obs, lon), 1)
    for r in range(regions):
        hit = jnp.broadcast_to(cell_t[:, r : r + 1], (obs, lon)) == index
        w = jnp.broadcast_to(weight_t[:, r : r + 1], (obs, lon))
        v = jnp.broadcast_to(value_t[:, r : r + 1], (obs, lon))
        dsum_ref[r : r + 1, :] = jnp.sum(jnp.where(hit, w, 0.0), axis=0, keepdims=True)
        vsum_ref[r : r + 1, :] = jnp.sum(jnp.where(hit, v, 0.0), axis=0, keepdims=True)


def per_cell(cells, values, weights, lon):
    regions, obs = cells.shape
    shape = jax.ShapeDtypeStruct((regions, lon), jnp.float32)
    return pl.pallas_call(
        cells_kernel,
        out_shape=(shape, shape),
        in_specs=whole(3),
        out_specs=tuple(whole(2)),
        cost_estimate=pl.CostEstimate(
            flops=4 * regions * obs * lon,
            bytes_accessed=4 * (3 * regions * obs + 2 * regions * lon),
            transcendentals=0,
        ),
        compiler_params=SMALL,
        name="per_cell",
    )(cells, values, weights)


def split(x):
    high = x.astype(jnp.bfloat16)
    low = (x - high.astype(jnp.float32)).astype(jnp.bfloat16)
    return high, low


def product(a, b, dims=((1,), (0,))):
    def dot(x, y):
        return lax.dot_general(x, y, (dims, ((), ())), preferred_element_type=jnp.float32)

    return dot(a[0], b[0]) + (dot(a[0], b[1]) + dot(a[1], b[0]))


def analysis_kernel(regions, parts, *refs):
    ens_refs, (dsum_ref, vsum_ref) = refs[:parts], refs[parts : parts + 2]
    out_refs = refs[parts + 2 :]
    share, lon = ens_refs[0].shape
    size = share * parts
    count = size // regions

    def over_members(x):
        if regions == 1:
            return jnp.sum(x, axis=0, keepdims=True)
        return jnp.sum(x.reshape(count, regions, x.shape[-1]), axis=0)

    def spread(x):
        if regions == 1:
            return jnp.broadcast_to(x, (size, x.shape[-1]))
        x = jnp.broadcast_to(x[None], (count, regions, x.shape[-1]))
        return x.reshape(size, x.shape[-1])

    ens = jnp.concatenate([ref[...] for ref in ens_refs], axis=0)
    dsum = dsum_ref[...]
    mean = over_members(ens) * (1.0 / count)
    pert = ens - spread(mean)
    pull = vsum_ref[...] - dsum * mean

    row = lax.broadcasted_iota(jnp.int32, (size, size), 0)
    col = lax.broadcasted_iota(jnp.int32, (size, size), 1)
    same = lax.rem(row, regions) == lax.rem(col, regions)
    one = jnp.where(row == col, 1.0, 0.0)

    pert_s = split(pert)
    gram = product(split(pert * spread(dsum)), pert_s, ((1,), (1,)))
    system = jnp.where(same, gram, 0.0) + (count - 1.0) * one
    total = over_members(jnp.sum(system * system, axis=1, keepdims=True))
    frob = jnp.sqrt(total)
    iterate = system * spread(1.0 / frob)
    iterate_s = split(iterate)
    inverse_s = None
    for sweep in range(SWEEPS):
        step = iterate if inverse_s is None else product(inverse_s, iterate_s)
        factor_s = split(1.5 * one - 0.5 * step)
        if sweep == SWEEPS - 1:
            break
        iterate_s = split(product(iterate_s, factor_s))
        inverse_s = factor_s if inverse_s is None else split(product(factor_s, inverse_s))
    part_s = split(product(inverse_s, pert_s))
    update = product(factor_s, part_s) * spread(lax.rsqrt(frob))
    gain = jnp.sum(update * spread(pull), axis=1, keepdims=True)
    shift = mean + over_members(update * gain)
    result = spread(shift) + jnp.sqrt(count - 1.0) * update
    for i, ref in enumerate(out_refs):
        ref[...] = result[i * share : (i + 1) * share]


def analysis(ens, dsum, vsum):
    parts = len(ens)
    share, lon = ens[0].shape
    size = share * parts
    regions = dsum.shape[0]
    return pl.pallas_call(
        functools.partial(analysis_kernel, regions, parts),
        out_shape=(jax.ShapeDtypeStruct((share, lon), jnp.float32),) * parts,
        in_specs=whole(parts + 2),
        out_specs=tuple(whole(parts)),
        cost_estimate=pl.CostEstimate(
            flops=48 * size * size * lon, bytes_accessed=8 * size * lon, transcendentals=0
        ),
        compiler_params=SMALL,
        name="analysis",
    )(*ens, dsum, vsum)


def place_rows_kernel(bands, crossed, got_ref, *refs):
    half_refs, out_ref, sems = refs[:-2], refs[-2], refs[-1]
    half = len(half_refs)
    members = out_ref.shape[0]
    chip, high, at_edge = place(bands)
    base = jnp.where(high, half, 0)
    copies = []
    for t, ref in enumerate(half_refs):
        r = row_of(chip, t, crossed)
        for source, row in ((ref.at[pl.ds(0, members)], base + r), (got_ref.at[t], half - base + r)):
            copies.append(
                pltpu.make_async_copy(source, out_ref.at[:, row], sems.at[len(copies)])
            )
    for copy in copies:
        copy.start()
    for copy in copies:
        copy.wait()


def place_rows(bands, crossed, got, halves, shape):
    half = len(halves)
    return pl.pallas_call(
        functools.partial(place_rows_kernel, bands, crossed),
        out_shape=jax.ShapeDtypeStruct(shape, jnp.float32),
        in_specs=whole(1 + half),
        out_specs=pl.BlockSpec(memory_space=pltpu.HBM),
        scratch_shapes=[pltpu.SemaphoreType.DMA((2 * half,))],
        compiler_params=SMALL,
        name="place_rows",
    )(got, *halves)


def body(state, zonal_wind, meridional_wind, obs_cell, obs_value, obs_weight):
    members, rows, levels, lon = state.shape
    groups = lax.axis_size("member")
    bands = lax.axis_size("lat")
    half = rows // 2
    chips = groups // 2
    regions = half * levels // chips
    crossed = chips == half and chips <= 4 and chips & (chips - 1) == 0

    def grouped(x):
        return x.reshape(groups, regions, x.shape[-1])

    partner = swap(state, groups, 1)
    own, zonal, merid, *tables = stage(
        bands,
        (state, zonal_wind, meridional_wind),
        (grouped(obs_cell), grouped(obs_value), grouped(obs_weight)),
    )
    message = edge_message(bands, own, partner, zonal, merid)
    halo = lax.ppermute(message, ("member", "lat"), halo_pairs(groups, bands))

    dsum, vsum = per_cell(*tables, lon)
    sent = forecast(bands, crossed, own, partner, halo, zonal, merid, dsum, vsum)
    same_core = [list(range(core, groups, 2)) for core in range(2)]

    def exchange(blocks):
        if crossed:
            return [blocks[0]] + [swap(b, groups, 2 * t) for t, b in enumerate(blocks) if t]
        return [
            lax.all_to_all(
                blocks[0], "member", 0, 0, tiled=True, axis_index_groups=same_core
            )
        ]

    if not crossed:
        field = jnp.stack(sent, axis=1).reshape(2 * members, chips, regions, lon)
        sent = [field.transpose(1, 0, 2, 3)]
    ensemble = exchange(sent)
    flat = [x.reshape(-1, lon) for x in ensemble]
    analysed = analysis(flat, dsum, vsum)
    back = exchange([x.reshape(e.shape) for x, e in zip(analysed, ensemble)])
    if not crossed:
        field = back[0].transpose(1, 0, 2, 3).reshape(2 * members, half, levels, lon)
        back = [field[:, t] for t in range(half)]
    got = swap(jnp.stack([b[members:] for b in back]), groups, 1)
    return place_rows(bands, crossed, got, back, state.shape)


def solution(mesh):
    in_specs = (
        P("member", "lat", None, None),
        P("lat", None, None),
        P("lat", None, None),
        P("lat", None, None),
        P("lat", None, None),
        P("lat", None, None),
    )
    out_specs = P("member", "lat", None, None)
    return jax.shard_map(body, mesh=mesh, in_specs=in_specs, out_specs=out_specs, check_vma=False)
```

```python
import functools

import jax
import jax.numpy as jnp
from jax import lax
from jax.experimental import pallas as pl
from jax.experimental.pallas import tpu as pltpu
from jax.sharding import PartitionSpec as P

SWEEPS = 3
step_size = 0.3
VM = pltpu.VMEM
SMALL = pltpu.CompilerParams(vmem_limit_bytes=12 * 2**20)


def whole(n):
    return [pl.BlockSpec(memory_space=VM)] * n


def place(bands):
    member, band = lax.axis_index("member"), lax.axis_index("lat")
    core, chip = lax.rem(member, 2), lax.div(member, 2)
    high = lax.rem(core + band, 2) == 0
    at_edge = jnp.where(high, band == bands - 1, band == 0)
    return chip, high, at_edge


def halo_pairs(groups, bands):
    pairs = []
    for member in range(groups):
        for band in range(bands):
            other, peer = band + (1 if (member + band) % 2 == 0 else -1), member
            if not 0 <= other < bands:
                other, peer = band, member ^ 2 if groups % 4 == 0 else member
            pairs.append((member * bands + band, peer * bands + other))
    return pairs


def swap(x, groups, distance):
    return lax.ppermute(x, "member", [(i, i ^ distance) for i in range(groups)])


def stage_kernel(bands, *refs):
    sources, targets, sems = refs[:6], refs[6:12], refs[12]
    chip, high, at_edge = place(bands)
    mine = jnp.where(high, sources[3].shape[0] // 2, 0) + chip
    sources = list(sources[:3]) + [ref.at[mine] for ref in sources[3:]]
    copies = [
        pltpu.make_async_copy(source, target, sems.at[i])
        for i, (source, target) in enumerate(zip(sources, targets))
    ]
    for copy in copies:
        copy.start()
    for copy in copies:
        copy.wait()


def stage(bands, fields, tables):
    shapes = [x.shape for x in fields] + [x.shape[1:] for x in tables]
    args = [pltpu.with_memory_space_constraint(x, pltpu.HBM) for x in (*fields, *tables)]
    return pl.pallas_call(
        functools.partial(stage_kernel, bands),
        out_shape=tuple(jax.ShapeDtypeStruct(n, x.dtype) for n, x in zip(shapes, args)),
        in_specs=[pl.BlockSpec(memory_space=pltpu.HBM)] * 6,
        out_specs=tuple(whole(6)),
        scratch_shapes=[pltpu.SemaphoreType.DMA((6,))],
        cost_estimate=pl.CostEstimate(flops=0, bytes_accessed=2**21, transcendentals=0),
        compiler_params=SMALL,
        name="stage",
    )(*args)


def edges_kernel(bands, own_ref, partner_ref, zonal_ref, merid_ref, out_ref):
    members, rows, levels, lon = own_ref.shape
    chip, high, at_edge = place(bands)
    first = jnp.where(high, rows - 2, 0)
    edge = jnp.where(high, rows - 1, 0)
    for m in range(2 * members):
        ref = own_ref if m < members else partner_ref
        out_ref[2 * m] = ref[m % members, first]
        out_ref[2 * m + 1] = ref[m % members, first + 1]
    out_ref[4 * members] = zonal_ref[edge]
    out_ref[4 * members + 1] = merid_ref[edge]


def edge_message(bands, own, partner, zonal, merid):
    members, rows, levels, lon = own.shape
    return pl.pallas_call(
        functools.partial(edges_kernel, bands),
        out_shape=jax.ShapeDtypeStruct((4 * members + 2, levels, lon), jnp.float32),
        in_specs=whole(4),
        out_specs=pl.BlockSpec(memory_space=VM),
        compiler_params=SMALL,
        name="edges",
    )(own, partner, zonal, merid)


def advance(south, middle, north, zonal, meridional):
    lon = middle.shape[-1]
    axis = middle.ndim - 1
    east = pltpu.roll(middle, lon - 1, axis)
    west = pltpu.roll(middle, 1, axis)
    return middle - step_size * (
        (zonal + middle) * (east - west) * 0.5 + meridional * (north - south) * 0.5
    )


def forecast_kernel(
    bands,
    crossed,
    own_ref,
    partner_ref,
    halo_ref,
    zonal_ref,
    merid_ref,
    dsum_ref,
    vsum_ref,
    *refs,
):
    out_refs, first_ref = refs[:-1], refs[-1]
    members, rows, levels, lon = own_ref.shape
    half = rows // 2
    chip, high, at_edge = place(bands)
    base = jnp.where(high, half, 0)

    def halo(i):
        return jnp.where(at_edge, 0.0, halo_ref[i])

    def winds(ref, outside):
        inside = [ref[base + r] for r in range(half)]
        before = jnp.where(high, ref[half - 1], outside)
        after = jnp.where(high, outside, ref[half])
        return [before, *inside, after]

    zonal = winds(zonal_ref, halo(4 * members))
    merid = winds(merid_ref, halo(4 * members + 1))
    for m in range(2 * members):
        ref, k = (own_ref if m < members else partner_ref), m % members
        outside = [halo(2 * m), halo(2 * m + 1)]
        q = [jnp.where(high, ref[k, half - 2 + i], outside[i]) for i in range(2)]
        q += [ref[k, base + r] for r in range(half)]
        q += [jnp.where(high, outside[i], ref[k, half + i]) for i in range(2)]
        for r in range(half + 2):
            first_ref[r, m] = advance(q[r], q[r + 1], q[r + 2], zonal[r], merid[r])
    for t in range(half):
        r = row_of(chip, t, crossed)
        zonal_row, merid_row = zonal_ref[base + r], merid_ref[base + r]
        for m in range(2 * members):
            out_refs[t][m] = advance(
                first_ref[r, m], first_ref[r + 1, m], first_ref[r + 2, m], zonal_row, merid_row
            )


def row_of(chip, t, crossed):
    return lax.bitwise_xor(chip, t) if crossed else t


def forecast(bands, crossed, own, partner, halo, zonal, merid, dsum, vsum):
    members, rows, levels, lon = own.shape
    half = rows // 2
    size = own.size
    shape = jax.ShapeDtypeStruct((2 * members, levels, lon), jnp.float32)
    return pl.pallas_call(
        functools.partial(forecast_kernel, bands, crossed),
        out_shape=(shape,) * half,
        in_specs=whole(5) + [pl.BlockSpec(memory_space=pl.ANY)] * 2,
        out_specs=tuple(whole(half)),
        scratch_shapes=[VM((half + 2, 2 * members, levels, lon), jnp.float32)],
        cost_estimate=pl.CostEstimate(
            flops=24 * size, bytes_accessed=8 * size, transcendentals=0
        ),
        compiler_params=SMALL,
        name="forecast",
    )(own, partner, halo, zonal, merid, dsum, vsum)


def cells_kernel(cell_ref, value_ref, weight_ref, dsum_ref, vsum_ref):
    regions, obs = cell_ref.shape
    lon = dsum_ref.shape[1]
    weight = weight_ref[...]
    cell_t = cell_ref[...].T
    weight_t = weight.T
    value_t = (weight * value_ref[...]).T
    index = lax.broadcasted_iota(jnp.int32, (obs, lon), 1)
    for r in range(regions):
        hit = jnp.broadcast_to(cell_t[:, r : r + 1], (obs, lon)) == index
        w = jnp.broadcast_to(weight_t[:, r : r + 1], (obs, lon))
        v = jnp.broadcast_to(value_t[:, r : r + 1], (obs, lon))
        dsum_ref[r : r + 1, :] = jnp.sum(jnp.where(hit, w, 0.0), axis=0, keepdims=True)
        vsum_ref[r : r + 1, :] = jnp.sum(jnp.where(hit, v, 0.0), axis=0, keepdims=True)


def per_cell(cells, values, weights, lon):
    regions, obs = cells.shape
    shape = jax.ShapeDtypeStruct((regions, lon), jnp.float32)
    return pl.pallas_call(
        cells_kernel,
        out_shape=(shape, shape),
        in_specs=whole(3),
        out_specs=tuple(whole(2)),
        cost_estimate=pl.CostEstimate(
            flops=4 * regions * obs * lon,
            bytes_accessed=4 * (3 * regions * obs + 2 * regions * lon),
            transcendentals=0,
        ),
        compiler_params=SMALL,
        name="per_cell",
    )(cells, values, weights)


def split(x):
    high = x.astype(jnp.bfloat16)
    low = (x - high.astype(jnp.float32)).astype(jnp.bfloat16)
    return high, low


def product(a, b, dims=((1,), (0,))):
    def dot(x, y):
        return lax.dot_general(x, y, (dims, ((), ())), preferred_element_type=jnp.float32)

    return dot(a[0], b[0]) + (dot(a[0], b[1]) + dot(a[1], b[0]))


def analysis_kernel(regions, parts, *refs):
    ens_refs, (dsum_ref, vsum_ref) = refs[:parts], refs[parts : parts + 2]
    out_refs = refs[parts + 2 :]
    share, lon = ens_refs[0].shape
    size = share * parts
    count = size // regions

    def over_members(x):
        if regions == 1:
            return jnp.sum(x, axis=0, keepdims=True)
        return jnp.sum(x.reshape(count, regions, x.shape[-1]), axis=0)

    def spread(x):
        if regions == 1:
            return jnp.broadcast_to(x, (size, x.shape[-1]))
        x = jnp.broadcast_to(x[None], (count, regions, x.shape[-1]))
        return x.reshape(size, x.shape[-1])

    ens = jnp.concatenate([ref[...] for ref in ens_refs], axis=0)
    dsum = dsum_ref[...]
    mean = over_members(ens) * (1.0 / count)
    pert = ens - spread(mean)
    pull = vsum_ref[...] - dsum * mean

    row = lax.broadcasted_iota(jnp.int32, (size, size), 0)
    col = lax.broadcasted_iota(jnp.int32, (size, size), 1)
    same = lax.rem(row, regions) == lax.rem(col, regions)
    one = jnp.where(row == col, 1.0, 0.0)

    pert_s = split(pert)
    gram = product(split(pert * spread(dsum)), pert_s, ((1,), (1,)))
    system = jnp.where(same, gram, 0.0) + (count - 1.0) * one
    total = over_members(jnp.sum(system * system, axis=1, keepdims=True))
    frob = jnp.sqrt(total)
    iterate = system * spread(1.0 / frob)
    iterate_s = split(iterate)
    inverse_s = None
    for sweep in range(SWEEPS):
        step = iterate if inverse_s is None else product(inverse_s, iterate_s)
        factor_s = split(1.5 * one - 0.5 * step)
        if sweep == SWEEPS - 1:
            break
        iterate_s = split(product(iterate_s, factor_s))
        inverse_s = factor_s if inverse_s is None else split(product(factor_s, inverse_s))
    part_s = split(product(inverse_s, pert_s))
    update = product(factor_s, part_s) * spread(lax.rsqrt(frob))
    gain = jnp.sum(update * spread(pull), axis=1, keepdims=True)
    shift = mean + over_members(update * gain)
    result = spread(shift) + jnp.sqrt(count - 1.0) * update
    for i, ref in enumerate(out_refs):
        ref[...] = result[i * share : (i + 1) * share]


def halves(x):
    return jnp.concatenate(split(x), axis=1)


def folded_product(a, b):
    n = b.shape[1] // 2
    both = jnp.concatenate([b, b], axis=0)
    out = jnp.dot(a, both, preferred_element_type=jnp.float32)
    return out[:, :n] + out[:, n:]


def folded_analysis_kernel(parts, *refs):
    ens_refs, (dsum_ref, vsum_ref) = refs[:parts], refs[parts : parts + 2]
    out_refs = refs[parts + 2 :]
    share, lon = ens_refs[0].shape
    count = share * parts // 8
    size = count * 4

    def low(n):
        return lax.broadcasted_iota(jnp.int32, (8, n), 0) < 4

    def turn(x):
        return pltpu.roll(x, 4, x.ndim - 2)

    def pattern(x):
        r, first = turn(x), low(x.shape[1])
        return jnp.where(first, x, r), jnp.where(first, r, x)

    def spread(x):
        n = x.shape[1]
        return jnp.broadcast_to(x[None], (count // 2, 8, n)).reshape(size, n)

    def over_members(x):
        total = jnp.sum(x.reshape(count // 2, 8, x.shape[1]), axis=0)
        return total + turn(total)

    ens = jnp.concatenate([ref[...] for ref in ens_refs], axis=0).reshape(count, 8, lon)
    dsum = dsum_ref[...]
    mean = jnp.sum(ens, axis=0) * (1.0 / count)
    pert = ens - mean[None]
    turned = turn(pert).reshape(count // 2, 2, 8, lon)
    pert = pert.reshape(count // 2, 2, 8, lon)
    first = low(lon)[None]
    groups = (
        jnp.where(first, pert[:, 0], turned[:, 1]).reshape(size, lon),
        jnp.where(first, turned[:, 0], pert[:, 1]).reshape(size, lon),
    )
    means = pattern(mean)
    dsums = pattern(dsum)
    pulls = pattern(vsum_ref[...] - dsum * mean)

    row = lax.broadcasted_iota(jnp.int32, (size, size), 0)
    col = lax.broadcasted_iota(jnp.int32, (size, size), 1)
    same = lax.rem(row, 4) == lax.rem(col, 4)
    one = jnp.where(row == col, 1.0, 0.0)

    def start(x, dsum):
        high, rest = split(x)
        w_high, w_low = split(x * spread(dsum))
        nt = (((1,), (1,)), ((), ()))
        main = lax.dot_general(
            w_high,
            jnp.concatenate([high, rest], axis=0),
            nt,
            preferred_element_type=jnp.float32,
        )
        more = lax.dot_general(w_low, high, nt, preferred_element_type=jnp.float32)
        gram = main[:, :size] + main[:, size:] + more
        system = jnp.where(same, gram, 0.0) + (count - 1.0) * one
        squares = jnp.sum(system * system, axis=1, keepdims=True)
        frob = jnp.sqrt(over_members(jnp.broadcast_to(squares, (size, size))))
        return system * spread(1.0 / frob), frob, jnp.concatenate([high, rest], axis=1)

    begun = [start(x, d) for x, d in zip(groups, dsums)]
    frobs = [b[1] for b in begun]
    perts = [b[2] for b in begun]
    steps = [b[0] for b in begun]
    iterates = [halves(x) for x in steps]
    inverses = None
    for sweep in range(SWEEPS):
        if inverses is not None:
            steps = [folded_product(z, y) for z, y in zip(inverses, iterates)]
        factors = [halves(1.5 * one - 0.5 * x) for x in steps]
        if sweep == SWEEPS - 1:
            break
        iterates = [halves(folded_product(y, f)) for y, f in zip(iterates, factors)]
        if inverses is None:
            inverses = factors
        else:
            inverses = [halves(folded_product(f, z)) for f, z in zip(factors, inverses)]
    partials = [halves(folded_product(z, x)) for z, x in zip(inverses, perts)]
    results = []
    for factor, part, frob, pull, mean_g in zip(factors, partials, frobs, pulls, means):
        scale = jnp.concatenate([spread(lax.rsqrt(frob))] * (lon // size), axis=1)
        update = folded_product(factor, part) * scale
        gain = jnp.sum(update * spread(pull), axis=1, keepdims=True)
        shift = mean_g + over_members(update * gain)
        results.append(
            (spread(shift) + jnp.sqrt(count - 1.0) * update).reshape(count // 2, 8, lon)
        )
    x, y = results
    even, odd = jnp.where(first, x, turn(y)), jnp.where(first, turn(x), y)
    for i in range(count // 2):
        ref, k = out_refs[2 * i // (share // 8)], (2 * i) % (share // 8)
        ref[8 * k : 8 * k + 8] = even[i]
        ref[8 * k + 8 : 8 * k + 16] = odd[i]


def analysis(ens, dsum, vsum):
    parts = len(ens)
    share, lon = ens[0].shape
    size = share * parts
    regions = dsum.shape[0]
    kernel = functools.partial(analysis_kernel, regions, parts)
    if regions == 8 and size == 256 and lon % 128 == 0 and share % 16 == 0:
        kernel = functools.partial(folded_analysis_kernel, parts)
    return pl.pallas_call(
        kernel,
        out_shape=(jax.ShapeDtypeStruct((share, lon), jnp.float32),) * parts,
        in_specs=whole(parts + 2),
        out_specs=tuple(whole(parts)),
        cost_estimate=pl.CostEstimate(
            flops=48 * size * size * lon, bytes_accessed=8 * size * lon, transcendentals=0
        ),
        compiler_params=SMALL,
        name="analysis",
    )(*ens, dsum, vsum)


def place_rows_kernel(bands, crossed, got_ref, *refs):
    half_refs, out_ref, sems = refs[:-2], refs[-2], refs[-1]
    half = len(half_refs)
    members = out_ref.shape[0]
    chip, high, at_edge = place(bands)
    base = jnp.where(high, half, 0)
    copies = []
    for t, ref in enumerate(half_refs):
        r = row_of(chip, t, crossed)
        for source, row in ((ref.at[pl.ds(0, members)], base + r), (got_ref.at[t], half - base + r)):
            copies.append(
                pltpu.make_async_copy(source, out_ref.at[:, row], sems.at[len(copies)])
            )
    for copy in copies:
        copy.start()
    for copy in copies:
        copy.wait()


def place_rows(bands, crossed, got, halves, shape):
    half = len(halves)
    return pl.pallas_call(
        functools.partial(place_rows_kernel, bands, crossed),
        out_shape=jax.ShapeDtypeStruct(shape, jnp.float32),
        in_specs=whole(1 + half),
        out_specs=pl.BlockSpec(memory_space=pltpu.HBM),
        scratch_shapes=[pltpu.SemaphoreType.DMA((2 * half,))],
        compiler_params=SMALL,
        name="place_rows",
    )(got, *halves)


def body(state, zonal_wind, meridional_wind, obs_cell, obs_value, obs_weight):
    members, rows, levels, lon = state.shape
    groups = lax.axis_size("member")
    bands = lax.axis_size("lat")
    half = rows // 2
    chips = groups // 2
    regions = half * levels // chips
    crossed = chips == half and chips <= 4 and chips & (chips - 1) == 0

    def grouped(x):
        return x.reshape(groups, regions, x.shape[-1])

    partner = swap(state, groups, 1)
    own, zonal, merid, *tables = stage(
        bands,
        (state, zonal_wind, meridional_wind),
        (grouped(obs_cell), grouped(obs_value), grouped(obs_weight)),
    )
    message = edge_message(bands, own, partner, zonal, merid)
    halo = lax.ppermute(message, ("member", "lat"), halo_pairs(groups, bands))

    dsum, vsum = per_cell(*tables, lon)
    sent = forecast(bands, crossed, own, partner, halo, zonal, merid, dsum, vsum)
    same_core = [list(range(core, groups, 2)) for core in range(2)]

    def exchange(blocks):
        if crossed:
            return [blocks[0]] + [swap(b, groups, 2 * t) for t, b in enumerate(blocks) if t]
        return [
            lax.all_to_all(
                blocks[0], "member", 0, 0, tiled=True, axis_index_groups=same_core
            )
        ]

    if not crossed:
        field = jnp.stack(sent, axis=1).reshape(2 * members, chips, regions, lon)
        sent = [field.transpose(1, 0, 2, 3)]
    ensemble = exchange(sent)
    flat = [x.reshape(-1, lon) for x in ensemble]
    analysed = analysis(flat, dsum, vsum)
    back = exchange([x.reshape(e.shape) for x, e in zip(analysed, ensemble)])
    if not crossed:
        field = back[0].transpose(1, 0, 2, 3).reshape(2 * members, half, levels, lon)
        back = [field[:, t] for t in range(half)]
    got = swap(jnp.stack([b[members:] for b in back]), groups, 1)
    return place_rows(bands, crossed, got, back, state.shape)


def solution(mesh):
    in_specs = (
        P("member", "lat", None, None),
        P("lat", None, None),
        P("lat", None, None),
        P("lat", None, None),
        P("lat", None, None),
        P("lat", None, None),
    )
    out_specs = P("member", "lat", None, None)
    return jax.shard_map(body, mesh=mesh, in_specs=in_specs, out_specs=out_specs, check_vma=False)
```

```python
import functools

import jax
import jax.numpy as jnp
from jax import lax
from jax.experimental import pallas as pl
from jax.experimental.pallas import tpu as pltpu
from jax.sharding import PartitionSpec as P

SWEEPS = 3
step_size = 0.3
VM = pltpu.VMEM
SMALL = pltpu.CompilerParams(vmem_limit_bytes=12 * 2**20)


def whole(n):
    return [pl.BlockSpec(memory_space=VM)] * n


def place(bands):
    member, band = lax.axis_index("member"), lax.axis_index("lat")
    core, chip = lax.rem(member, 2), lax.div(member, 2)
    high = lax.rem(core + band, 2) == 0
    at_edge = jnp.where(high, band == bands - 1, band == 0)
    return chip, high, at_edge


def halo_pairs(groups, bands):
    pairs = []
    for member in range(groups):
        for band in range(bands):
            other, peer = band + (1 if (member + band) % 2 == 0 else -1), member
            if not 0 <= other < bands:
                other, peer = band, member ^ 2 if groups % 4 == 0 else member
            pairs.append((member * bands + band, peer * bands + other))
    return pairs


def swap(x, groups, distance):
    return lax.ppermute(x, "member", [(i, i ^ distance) for i in range(groups)])


def stage_kernel(bands, *refs):
    sources, targets, sems = refs[:6], refs[6:12], refs[12]
    chip, high, at_edge = place(bands)
    mine = jnp.where(high, sources[3].shape[0] // 2, 0) + chip
    sources = list(sources[:3]) + [ref.at[mine] for ref in sources[3:]]
    copies = [
        pltpu.make_async_copy(source, target, sems.at[i])
        for i, (source, target) in enumerate(zip(sources, targets))
    ]
    for copy in copies:
        copy.start()
    for copy in copies:
        copy.wait()


def stage(bands, fields, tables):
    shapes = [x.shape for x in fields] + [x.shape[1:] for x in tables]
    args = [pltpu.with_memory_space_constraint(x, pltpu.HBM) for x in (*fields, *tables)]
    return pl.pallas_call(
        functools.partial(stage_kernel, bands),
        out_shape=tuple(jax.ShapeDtypeStruct(n, x.dtype) for n, x in zip(shapes, args)),
        in_specs=[pl.BlockSpec(memory_space=pltpu.HBM)] * 6,
        out_specs=tuple(whole(6)),
        scratch_shapes=[pltpu.SemaphoreType.DMA((6,))],
        cost_estimate=pl.CostEstimate(flops=0, bytes_accessed=2**21, transcendentals=0),
        compiler_params=SMALL,
        name="stage",
    )(*args)


def edges_kernel(bands, own_ref, partner_ref, zonal_ref, merid_ref, out_ref):
    members, rows, levels, lon = own_ref.shape
    chip, high, at_edge = place(bands)
    first = jnp.where(high, rows - 2, 0)
    edge = jnp.where(high, rows - 1, 0)
    for m in range(2 * members):
        ref = own_ref if m < members else partner_ref
        out_ref[2 * m] = ref[m % members, first]
        out_ref[2 * m + 1] = ref[m % members, first + 1]
    out_ref[4 * members] = zonal_ref[edge]
    out_ref[4 * members + 1] = merid_ref[edge]


def edge_message(bands, own, partner, zonal, merid):
    members, rows, levels, lon = own.shape
    return pl.pallas_call(
        functools.partial(edges_kernel, bands),
        out_shape=jax.ShapeDtypeStruct((4 * members + 2, levels, lon), jnp.float32),
        in_specs=whole(4),
        out_specs=pl.BlockSpec(memory_space=VM),
        compiler_params=SMALL,
        name="edges",
    )(own, partner, zonal, merid)


def advance(south, middle, north, zonal, meridional):
    lon = middle.shape[-1]
    axis = middle.ndim - 1
    east = pltpu.roll(middle, lon - 1, axis)
    west = pltpu.roll(middle, 1, axis)
    return middle - step_size * (
        (zonal + middle) * (east - west) * 0.5 + meridional * (north - south) * 0.5
    )


def forecast_kernel(
    bands,
    crossed,
    own_ref,
    partner_ref,
    halo_ref,
    zonal_ref,
    merid_ref,
    dsum_ref,
    vsum_ref,
    *refs,
):
    out_refs, first_ref = refs[:-1], refs[-1]
    members, rows, levels, lon = own_ref.shape
    half = rows // 2
    chip, high, at_edge = place(bands)
    base = jnp.where(high, half, 0)

    def halo(i):
        return jnp.where(at_edge, 0.0, halo_ref[i])

    def winds(ref, outside):
        inside = [ref[base + r] for r in range(half)]
        before = jnp.where(high, ref[half - 1], outside)
        after = jnp.where(high, outside, ref[half])
        return [before, *inside, after]

    zonal = winds(zonal_ref, halo(4 * members))
    merid = winds(merid_ref, halo(4 * members + 1))
    for m in range(2 * members):
        ref, k = (own_ref if m < members else partner_ref), m % members
        outside = [halo(2 * m), halo(2 * m + 1)]
        q = [jnp.where(high, ref[k, half - 2 + i], outside[i]) for i in range(2)]
        q += [ref[k, base + r] for r in range(half)]
        q += [jnp.where(high, outside[i], ref[k, half + i]) for i in range(2)]
        for r in range(half + 2):
            first_ref[r, m] = advance(q[r], q[r + 1], q[r + 2], zonal[r], merid[r])
    for t in range(half):
        r = row_of(chip, t, crossed)
        zonal_row, merid_row = zonal_ref[base + r], merid_ref[base + r]
        for m in range(2 * members):
            out_refs[t][m] = advance(
                first_ref[r, m], first_ref[r + 1, m], first_ref[r + 2, m], zonal_row, merid_row
            )


def row_of(chip, t, crossed):
    return lax.bitwise_xor(chip, t) if crossed else t


def forecast(bands, crossed, own, partner, halo, zonal, merid, dsum, vsum):
    members, rows, levels, lon = own.shape
    half = rows // 2
    size = own.size
    shape = jax.ShapeDtypeStruct((2 * members, levels, lon), jnp.float32)
    return pl.pallas_call(
        functools.partial(forecast_kernel, bands, crossed),
        out_shape=(shape,) * half,
        in_specs=whole(5) + [pl.BlockSpec(memory_space=pl.ANY)] * 2,
        out_specs=tuple(whole(half)),
        scratch_shapes=[VM((half + 2, 2 * members, levels, lon), jnp.float32)],
        cost_estimate=pl.CostEstimate(
            flops=24 * size, bytes_accessed=8 * size, transcendentals=0
        ),
        compiler_params=SMALL,
        name="forecast",
    )(own, partner, halo, zonal, merid, dsum, vsum)


def cells_kernel(cell_ref, value_ref, weight_ref, dsum_ref, vsum_ref):
    regions, obs = cell_ref.shape
    lon = dsum_ref.shape[1]
    weight = weight_ref[...]
    cell_t = cell_ref[...].T
    weight_t = weight.T
    value_t = (weight * value_ref[...]).T
    index = lax.broadcasted_iota(jnp.int32, (obs, lon), 1)
    for r in range(regions):
        hit = jnp.broadcast_to(cell_t[:, r : r + 1], (obs, lon)) == index
        w = jnp.broadcast_to(weight_t[:, r : r + 1], (obs, lon))
        v = jnp.broadcast_to(value_t[:, r : r + 1], (obs, lon))
        dsum_ref[r : r + 1, :] = jnp.sum(jnp.where(hit, w, 0.0), axis=0, keepdims=True)
        vsum_ref[r : r + 1, :] = jnp.sum(jnp.where(hit, v, 0.0), axis=0, keepdims=True)


def per_cell(cells, values, weights, lon):
    regions, obs = cells.shape
    shape = jax.ShapeDtypeStruct((regions, lon), jnp.float32)
    return pl.pallas_call(
        cells_kernel,
        out_shape=(shape, shape),
        in_specs=whole(3),
        out_specs=tuple(whole(2)),
        cost_estimate=pl.CostEstimate(
            flops=4 * regions * obs * lon,
            bytes_accessed=4 * (3 * regions * obs + 2 * regions * lon),
            transcendentals=0,
        ),
        compiler_params=SMALL,
        name="per_cell",
    )(cells, values, weights)


def split(x):
    high = x.astype(jnp.bfloat16)
    low = (x - high.astype(jnp.float32)).astype(jnp.bfloat16)
    return high, low


def product(a, b, dims=((1,), (0,))):
    def dot(x, y):
        return lax.dot_general(x, y, (dims, ((), ())), preferred_element_type=jnp.float32)

    return dot(a[0], b[0]) + (dot(a[0], b[1]) + dot(a[1], b[0]))


def analysis_kernel(regions, parts, *refs):
    ens_refs, (dsum_ref, vsum_ref) = refs[:parts], refs[parts : parts + 2]
    out_refs = refs[parts + 2 :]
    share, lon = ens_refs[0].shape
    size = share * parts
    count = size // regions

    def over_members(x):
        if regions == 1:
            return jnp.sum(x, axis=0, keepdims=True)
        return jnp.sum(x.reshape(count, regions, x.shape[-1]), axis=0)

    def spread(x):
        if regions == 1:
            return jnp.broadcast_to(x, (size, x.shape[-1]))
        x = jnp.broadcast_to(x[None], (count, regions, x.shape[-1]))
        return x.reshape(size, x.shape[-1])

    ens = jnp.concatenate([ref[...] for ref in ens_refs], axis=0)
    dsum = dsum_ref[...]
    mean = over_members(ens) * (1.0 / count)
    pert = ens - spread(mean)
    pull = vsum_ref[...] - dsum * mean

    row = lax.broadcasted_iota(jnp.int32, (size, size), 0)
    col = lax.broadcasted_iota(jnp.int32, (size, size), 1)
    same = lax.rem(row, regions) == lax.rem(col, regions)
    one = jnp.where(row == col, 1.0, 0.0)

    pert_s = split(pert)
    gram = product(split(pert * spread(dsum)), pert_s, ((1,), (1,)))
    system = jnp.where(same, gram, 0.0) + (count - 1.0) * one
    total = over_members(jnp.sum(system * system, axis=1, keepdims=True))
    frob = jnp.sqrt(total)
    iterate = system * spread(1.0 / frob)
    iterate_s = split(iterate)
    inverse_s = None
    for sweep in range(SWEEPS):
        step = iterate if inverse_s is None else product(inverse_s, iterate_s)
        factor_s = split(1.5 * one - 0.5 * step)
        if sweep == SWEEPS - 1:
            break
        iterate_s = split(product(iterate_s, factor_s))
        inverse_s = factor_s if inverse_s is None else split(product(factor_s, inverse_s))
    part_s = split(product(inverse_s, pert_s))
    update = product(factor_s, part_s) * spread(lax.rsqrt(frob))
    gain = jnp.sum(update * spread(pull), axis=1, keepdims=True)
    shift = mean + over_members(update * gain)
    result = spread(shift) + jnp.sqrt(count - 1.0) * update
    for i, ref in enumerate(out_refs):
        ref[...] = result[i * share : (i + 1) * share]


def halves(x):
    return jnp.concatenate(split(x), axis=1)


def folded_product(a, b):
    n = b.shape[1] // 2
    both = jnp.concatenate([b, b], axis=0)
    out = jnp.dot(a, both, preferred_element_type=jnp.float32)
    return out[:, :n] + out[:, n:]


def folded_analysis_kernel(parts, *refs):
    ens_refs, (dsum_ref, vsum_ref) = refs[:parts], refs[parts : parts + 2]
    out_refs = refs[parts + 2 :]
    share, lon = ens_refs[0].shape
    count = share * parts // 8
    size = count * 4

    def low(n):
        return lax.broadcasted_iota(jnp.int32, (8, n), 0) < 4

    def turn(x):
        return pltpu.roll(x, 4, x.ndim - 2)

    def pattern(x):
        r, first = turn(x), low(x.shape[1])
        return jnp.where(first, x, r), jnp.where(first, r, x)

    def spread(x):
        n = x.shape[1]
        return jnp.broadcast_to(x[None], (count // 2, 8, n)).reshape(size, n)

    def over_members(x):
        total = jnp.sum(x.reshape(count // 2, 8, x.shape[1]), axis=0)
        return total + turn(total)

    ens = jnp.concatenate([ref[...] for ref in ens_refs], axis=0).reshape(count, 8, lon)
    dsum = dsum_ref[...]
    mean = jnp.sum(ens, axis=0) * (1.0 / count)
    pert = ens - mean[None]
    turned = turn(pert).reshape(count // 2, 2, 8, lon)
    pert = pert.reshape(count // 2, 2, 8, lon)
    first = low(lon)[None]
    groups = (
        jnp.where(first, pert[:, 0], turned[:, 1]).reshape(size, lon),
        jnp.where(first, turned[:, 0], pert[:, 1]).reshape(size, lon),
    )
    means = pattern(mean)
    dsums = pattern(dsum)
    pulls = pattern(vsum_ref[...] - dsum * mean)

    row = lax.broadcasted_iota(jnp.int32, (size, size), 0)
    col = lax.broadcasted_iota(jnp.int32, (size, size), 1)
    same = lax.rem(row, 4) == lax.rem(col, 4)
    one = jnp.where(row == col, 1.0, 0.0)

    def start(x, dsum):
        high, rest = split(x)
        w_high, w_low = split(x * spread(dsum))
        nt = (((1,), (1,)), ((), ()))
        main = lax.dot_general(
            w_high,
            jnp.concatenate([high, rest], axis=0),
            nt,
            preferred_element_type=jnp.float32,
        )
        more = lax.dot_general(w_low, high, nt, preferred_element_type=jnp.float32)
        gram = main[:, :size] + main[:, size:] + more
        system = jnp.where(same, gram, 0.0) + (count - 1.0) * one
        squares = jnp.sum(system * system, axis=1, keepdims=True)
        frob = jnp.sqrt(over_members(jnp.broadcast_to(squares, (size, size))))
        return system * spread(1.0 / frob), frob, jnp.concatenate([high, rest], axis=1)

    begun = [start(x, d) for x, d in zip(groups, dsums)]
    frobs = [b[1] for b in begun]
    perts = [b[2] for b in begun]
    steps = [b[0] for b in begun]
    iterates = [halves(x) for x in steps]
    inverses = None
    for sweep in range(SWEEPS):
        if inverses is not None:
            steps = [folded_product(z, y) for z, y in zip(inverses, iterates)]
        factors = [halves(1.5 * one - 0.5 * x) for x in steps]
        if sweep == SWEEPS - 1:
            break
        iterates = [halves(folded_product(y, f)) for y, f in zip(iterates, factors)]
        if inverses is None:
            inverses = factors
        else:
            inverses = [halves(folded_product(f, z)) for f, z in zip(factors, inverses)]
    partials = [halves(folded_product(z, x)) for z, x in zip(inverses, perts)]
    results = []
    for factor, part, frob, pull, mean_g in zip(factors, partials, frobs, pulls, means):
        scale = jnp.concatenate([spread(lax.rsqrt(frob))] * (lon // size), axis=1)
        update = folded_product(factor, part) * scale
        gain = jnp.sum(update * spread(pull), axis=1, keepdims=True)
        shift = mean_g + over_members(update * gain)
        results.append(
            (spread(shift) + jnp.sqrt(count - 1.0) * update).reshape(count // 2, 8, lon)
        )
    x, y = results
    even, odd = jnp.where(first, x, turn(y)), jnp.where(first, turn(x), y)
    for i in range(count // 2):
        ref, k = out_refs[2 * i // (share // 8)], (2 * i) % (share // 8)
        ref[8 * k : 8 * k + 8] = even[i]
        ref[8 * k + 8 : 8 * k + 16] = odd[i]


def analysis(ens, dsum, vsum):
    parts = len(ens)
    share, lon = ens[0].shape
    size = share * parts
    regions = dsum.shape[0]
    kernel = functools.partial(analysis_kernel, regions, parts)
    if regions == 8 and size == 256 and lon % 128 == 0 and share % 16 == 0:
        kernel = functools.partial(folded_analysis_kernel, parts)
    return pl.pallas_call(
        kernel,
        out_shape=(jax.ShapeDtypeStruct((share, lon), jnp.float32),) * parts,
        in_specs=whole(parts + 2),
        out_specs=tuple(whole(parts)),
        cost_estimate=pl.CostEstimate(
            flops=48 * size * size * lon, bytes_accessed=8 * size * lon, transcendentals=0
        ),
        compiler_params=SMALL,
        name="analysis",
    )(*ens, dsum, vsum)


def place_rows_kernel(bands, crossed, *refs):
    out_ref, sems = refs[-2:]
    half = out_ref.shape[1] // 2
    got_refs, half_refs = refs[:half], refs[half : 2 * half]
    members = out_ref.shape[0]
    chip, high, at_edge = place(bands)
    base = jnp.where(high, half, 0)
    copies = []
    for t, ref in enumerate(half_refs):
        r = row_of(chip, t, crossed)
        for source, row in ((ref.at[pl.ds(0, members)], base + r), (got_refs[t], half - base + r)):
            copies.append(
                pltpu.make_async_copy(source, out_ref.at[:, row], sems.at[len(copies)])
            )
    for copy in copies:
        copy.start()
    for copy in copies:
        copy.wait()


def place_rows(bands, crossed, got, halves, shape):
    half = len(halves)
    return pl.pallas_call(
        functools.partial(place_rows_kernel, bands, crossed),
        out_shape=jax.ShapeDtypeStruct(shape, jnp.float32),
        in_specs=whole(2 * half),
        out_specs=pl.BlockSpec(memory_space=pltpu.HBM),
        scratch_shapes=[pltpu.SemaphoreType.DMA((2 * half,))],
        compiler_params=SMALL,
        name="place_rows",
    )(*got, *halves)


def body(state, zonal_wind, meridional_wind, obs_cell, obs_value, obs_weight):
    members, rows, levels, lon = state.shape
    groups = lax.axis_size("member")
    bands = lax.axis_size("lat")
    half = rows // 2
    chips = groups // 2
    regions = half * levels // chips
    crossed = chips == half and chips <= 4 and chips & (chips - 1) == 0

    def grouped(x):
        return x.reshape(groups, regions, x.shape[-1])

    partner = swap(state, groups, 1)
    own, zonal, merid, *tables = stage(
        bands,
        (state, zonal_wind, meridional_wind),
        (grouped(obs_cell), grouped(obs_value), grouped(obs_weight)),
    )
    message = edge_message(bands, own, partner, zonal, merid)
    halo = lax.ppermute(message, ("member", "lat"), halo_pairs(groups, bands))

    dsum, vsum = per_cell(*tables, lon)
    sent = forecast(bands, crossed, own, partner, halo, zonal, merid, dsum, vsum)
    same_core = [list(range(core, groups, 2)) for core in range(2)]

    def exchange(blocks):
        if crossed:
            return [blocks[0]] + [swap(b, groups, 2 * t) for t, b in enumerate(blocks) if t]
        return [
            lax.all_to_all(
                blocks[0], "member", 0, 0, tiled=True, axis_index_groups=same_core
            )
        ]

    if not crossed:
        field = jnp.stack(sent, axis=1).reshape(2 * members, chips, regions, lon)
        sent = [field.transpose(1, 0, 2, 3)]
    ensemble = exchange(sent)
    flat = [x.reshape(-1, lon) for x in ensemble]
    analysed = analysis(flat, dsum, vsum)
    back = exchange([x.reshape(e.shape) for x, e in zip(analysed, ensemble)])
    if not crossed:
        field = back[0].transpose(1, 0, 2, 3).reshape(2 * members, half, levels, lon)
        back = [field[:, t] for t in range(half)]
    got = [swap(b[members:], groups, 1) for b in back]
    return place_rows(bands, crossed, got, back, state.shape)


def solution(mesh):
    in_specs = (
        P("member", "lat", None, None),
        P("lat", None, None),
        P("lat", None, None),
        P("lat", None, None),
        P("lat", None, None),
        P("lat", None, None),
    )
    out_specs = P("member", "lat", None, None)
    return jax.shard_map(body, mesh=mesh, in_specs=in_specs, out_specs=out_specs, check_vma=False)
```

```python
import functools

import jax
import jax.numpy as jnp
from jax import lax
from jax.experimental import pallas as pl
from jax.experimental.pallas import tpu as pltpu
from jax.sharding import PartitionSpec as P

SWEEPS = 3
step_size = 0.3
VM = pltpu.VMEM
SMALL = pltpu.CompilerParams(vmem_limit_bytes=12 * 2**20)


def whole(n):
    return [pl.BlockSpec(memory_space=VM)] * n


def place(bands):
    member, band = lax.axis_index("member"), lax.axis_index("lat")
    core, chip = lax.rem(member, 2), lax.div(member, 2)
    high = lax.rem(core + band, 2) == 0
    at_edge = jnp.where(high, band == bands - 1, band == 0)
    return chip, high, at_edge


def row_at(high, rows, e):
    return jnp.where(high, rows - 1 - e, e)


def halo_pairs(groups, bands):
    pairs = []
    for member in range(groups):
        for band in range(bands):
            other, peer = band + (1 if (member + band) % 2 == 0 else -1), member
            if not 0 <= other < bands:
                other, peer = band, member ^ 2 if groups % 4 == 0 else member
            pairs.append((member * bands + band, peer * bands + other))
    return pairs


def swap(x, groups, distance):
    return lax.ppermute(x, "member", [(i, i ^ distance) for i in range(groups)])


def stage_kernel(bands, *refs):
    sources, targets, sems = refs[:6], refs[6:12], refs[12]
    chip, high, at_edge = place(bands)
    rows, levels = sources[0].shape[1:3]
    per_row = levels // sources[3].shape[1]
    mine = row_at(high, rows, lax.div(chip, per_row)) * per_row + lax.rem(chip, per_row)
    sources = list(sources[:3]) + [ref.at[mine] for ref in sources[3:]]
    copies = [
        pltpu.make_async_copy(source, target, sems.at[i])
        for i, (source, target) in enumerate(zip(sources, targets))
    ]
    for copy in copies:
        copy.start()
    for copy in copies:
        copy.wait()


def stage(bands, fields, tables):
    shapes = [x.shape for x in fields] + [x.shape[1:] for x in tables]
    args = [pltpu.with_memory_space_constraint(x, pltpu.HBM) for x in (*fields, *tables)]
    return pl.pallas_call(
        functools.partial(stage_kernel, bands),
        out_shape=tuple(jax.ShapeDtypeStruct(n, x.dtype) for n, x in zip(shapes, args)),
        in_specs=[pl.BlockSpec(memory_space=pltpu.HBM)] * 6,
        out_specs=tuple(whole(6)),
        scratch_shapes=[pltpu.SemaphoreType.DMA((6,))],
        cost_estimate=pl.CostEstimate(flops=0, bytes_accessed=2**21, transcendentals=0),
        compiler_params=SMALL,
        name="stage",
    )(*args)


def edges_kernel(bands, own_ref, partner_ref, zonal_ref, merid_ref, out_ref):
    members, rows, levels, lon = own_ref.shape
    chip, high, at_edge = place(bands)
    edge = row_at(high, rows, 0)
    for m in range(2 * members):
        ref = own_ref if m < members else partner_ref
        out_ref[2 * m] = ref[m % members, edge]
        out_ref[2 * m + 1] = ref[m % members, row_at(high, rows, 1)]
    out_ref[4 * members] = zonal_ref[edge]
    out_ref[4 * members + 1] = merid_ref[edge]


def edge_message(bands, own, partner, zonal, merid):
    members, rows, levels, lon = own.shape
    return pl.pallas_call(
        functools.partial(edges_kernel, bands),
        out_shape=jax.ShapeDtypeStruct((4 * members + 2, levels, lon), jnp.float32),
        in_specs=whole(4),
        out_specs=pl.BlockSpec(memory_space=VM),
        compiler_params=SMALL,
        name="edges",
    )(own, partner, zonal, merid)


def advance(before, middle, after, zonal, inward):
    lon = middle.shape[-1]
    axis = middle.ndim - 1
    east = pltpu.roll(middle, lon - 1, axis)
    west = pltpu.roll(middle, 1, axis)
    change = (zonal + middle) * (east - west) + inward * (after - before)
    return middle - (0.5 * step_size) * change


def wind_row(high, rows, e, zonal_ref, merid_ref):
    row = row_at(high, rows, e)
    return zonal_ref[row], jnp.where(high, -merid_ref[row], merid_ref[row])


def row_of(chip, t, crossed):
    return lax.bitwise_xor(chip, t) if crossed else t


def on(condition):
    if isinstance(condition, bool):
        return (lambda f: f()) if condition else (lambda f: None)
    return pl.when(condition)


def inner_kernel(bands, crossed, own_ref, partner_ref, zonal_ref, merid_ref, *refs):
    first_ref, out_refs = refs[0], refs[1:]
    members, rows, levels, lon = own_ref.shape
    half = rows // 2
    chip, high, at_edge = place(bands)
    wind = [wind_row(high, rows, e, zonal_ref, merid_ref) for e in range(1, half + 1)]
    for m in range(2 * members):
        ref, k = (own_ref if m < members else partner_ref), m % members
        q = [ref[k, row_at(high, rows, e)] for e in range(half + 2)]
        for e in range(1, half + 1):
            first_ref[e - 1, m] = advance(q[e - 1], q[e], q[e + 1], *wind[e - 1])
    for t, out_ref in enumerate(out_refs):
        e = row_of(chip, t, crossed)

        @on(e >= 2)
        def _(e=e, out_ref=out_ref):
            wind = wind_row(high, rows, e, zonal_ref, merid_ref)
            for m in range(2 * members):
                out_ref[m] = advance(
                    first_ref[e - 2, m], first_ref[e - 1, m], first_ref[e, m], *wind
                )


def edge_kernel(bands, crossed, own_ref, partner_ref, halo_ref, zonal_ref, merid_ref, *refs):
    members, rows, levels, lon = own_ref.shape
    half = rows // 2
    inner_ref, done_refs = refs[0], refs[1 : 1 + half]
    out_refs, first_ref = refs[-1 - half : -1], refs[-1]
    chip, high, at_edge = place(bands)

    def halo(i):
        return jnp.where(at_edge, 0.0, halo_ref[i])

    merid = halo(4 * members + 1)
    outside = halo(4 * members), jnp.where(high, -merid, merid)
    edge = wind_row(high, rows, 0, zonal_ref, merid_ref)
    for m in range(2 * members):
        ref, k = (own_ref if m < members else partner_ref), m % members
        q = [halo(2 * m + 1), halo(2 * m)]
        q += [ref[k, row_at(high, rows, e)] for e in range(2)]
        first_ref[0, m] = advance(q[0], q[1], q[2], *outside)
        first_ref[1, m] = advance(q[1], q[2], q[3], *edge)
        first_ref[2, m] = inner_ref[0, m]
        first_ref[3, m] = inner_ref[1, m]
    for t, (done_ref, out_ref) in enumerate(zip(done_refs, out_refs)):
        e = row_of(chip, t, crossed)

        @on(e >= 2)
        def _(done_ref=done_ref, out_ref=out_ref):
            out_ref[...] = done_ref[...]

        @on(e < 2)
        def _(e=e, out_ref=out_ref):
            wind = wind_row(high, rows, e, zonal_ref, merid_ref)
            for m in range(2 * members):
                out_ref[m] = advance(
                    first_ref[e, m], first_ref[e + 1, m], first_ref[e + 2, m], *wind
                )


def forecast_inner(bands, crossed, own, partner, zonal, merid):
    members, rows, levels, lon = own.shape
    half = rows // 2
    size = own.size
    block = (2 * members, levels, lon)
    return pl.pallas_call(
        functools.partial(inner_kernel, bands, crossed),
        out_shape=(jax.ShapeDtypeStruct((half, *block), jnp.float32),)
        + (jax.ShapeDtypeStruct(block, jnp.float32),) * half,
        in_specs=whole(4),
        out_specs=tuple(whole(half + 1)),
        cost_estimate=pl.CostEstimate(
            flops=16 * size, bytes_accessed=8 * size, transcendentals=0
        ),
        compiler_params=SMALL,
        name="forecast_inner",
    )(own, partner, zonal, merid)


def forecast_edge(bands, crossed, own, partner, halo, zonal, merid, inner, sent, dsum, vsum):
    members, rows, levels, lon = own.shape
    half = rows // 2
    size = own.size
    block = (2 * members, levels, lon)
    return pl.pallas_call(
        functools.partial(edge_kernel, bands, crossed),
        out_shape=(jax.ShapeDtypeStruct(block, jnp.float32),) * half,
        in_specs=whole(6 + half) + [pl.BlockSpec(memory_space=pl.ANY)] * 2,
        out_specs=tuple(whole(half)),
        scratch_shapes=[VM((4, *block), jnp.float32)],
        cost_estimate=pl.CostEstimate(
            flops=8 * size, bytes_accessed=4 * size, transcendentals=0
        ),
        compiler_params=SMALL,
        name="forecast_edge",
    )(own, partner, halo, zonal, merid, inner, *sent, dsum, vsum)


def cells_kernel(cell_ref, value_ref, weight_ref, dsum_ref, vsum_ref):
    regions, obs = cell_ref.shape
    lon = dsum_ref.shape[1]
    weight = weight_ref[...]
    cell_t = cell_ref[...].T
    weight_t = weight.T
    value_t = (weight * value_ref[...]).T
    index = lax.broadcasted_iota(jnp.int32, (obs, lon), 1)
    for r in range(regions):
        hit = jnp.broadcast_to(cell_t[:, r : r + 1], (obs, lon)) == index
        w = jnp.broadcast_to(weight_t[:, r : r + 1], (obs, lon))
        v = jnp.broadcast_to(value_t[:, r : r + 1], (obs, lon))
        dsum_ref[r : r + 1, :] = jnp.sum(jnp.where(hit, w, 0.0), axis=0, keepdims=True)
        vsum_ref[r : r + 1, :] = jnp.sum(jnp.where(hit, v, 0.0), axis=0, keepdims=True)


def per_cell(cells, values, weights, lon):
    regions, obs = cells.shape
    shape = jax.ShapeDtypeStruct((regions, lon), jnp.float32)
    return pl.pallas_call(
        cells_kernel,
        out_shape=(shape, shape),
        in_specs=whole(3),
        out_specs=tuple(whole(2)),
        cost_estimate=pl.CostEstimate(
            flops=4 * regions * obs * lon,
            bytes_accessed=4 * (3 * regions * obs + 2 * regions * lon),
            transcendentals=0,
        ),
        compiler_params=SMALL,
        name="per_cell",
    )(cells, values, weights)


def split(x):
    high = x.astype(jnp.bfloat16)
    low = (x - high.astype(jnp.float32)).astype(jnp.bfloat16)
    return high, low


def product(a, b, dims=((1,), (0,))):
    def dot(x, y):
        return lax.dot_general(x, y, (dims, ((), ())), preferred_element_type=jnp.float32)

    return dot(a[0], b[0]) + (dot(a[0], b[1]) + dot(a[1], b[0]))


def analysis_kernel(regions, parts, *refs):
    ens_refs, (dsum_ref, vsum_ref) = refs[:parts], refs[parts : parts + 2]
    out_refs = refs[parts + 2 :]
    share, lon = ens_refs[0].shape
    size = share * parts
    count = size // regions

    def over_members(x):
        if regions == 1:
            return jnp.sum(x, axis=0, keepdims=True)
        return jnp.sum(x.reshape(count, regions, x.shape[-1]), axis=0)

    def spread(x):
        if regions == 1:
            return jnp.broadcast_to(x, (size, x.shape[-1]))
        x = jnp.broadcast_to(x[None], (count, regions, x.shape[-1]))
        return x.reshape(size, x.shape[-1])

    ens = jnp.concatenate([ref[...] for ref in ens_refs], axis=0)
    dsum = dsum_ref[...]
    mean = over_members(ens) * (1.0 / count)
    pert = ens - spread(mean)
    pull = vsum_ref[...] - dsum * mean

    row = lax.broadcasted_iota(jnp.int32, (size, size), 0)
    col = lax.broadcasted_iota(jnp.int32, (size, size), 1)
    same = lax.rem(row, regions) == lax.rem(col, regions)
    one = jnp.where(row == col, 1.0, 0.0)

    pert_s = split(pert)
    gram = product(split(pert * spread(dsum)), pert_s, ((1,), (1,)))
    system = jnp.where(same, gram, 0.0) + (count - 1.0) * one
    total = over_members(jnp.sum(system * system, axis=1, keepdims=True))
    frob = jnp.sqrt(total)
    iterate = system * spread(1.0 / frob)
    iterate_s = split(iterate)
    inverse_s = None
    for sweep in range(SWEEPS):
        step = iterate if inverse_s is None else product(inverse_s, iterate_s)
        factor_s = split(1.5 * one - 0.5 * step)
        if sweep == SWEEPS - 1:
            break
        iterate_s = split(product(iterate_s, factor_s))
        inverse_s = factor_s if inverse_s is None else split(product(factor_s, inverse_s))
    part_s = split(product(inverse_s, pert_s))
    update = product(factor_s, part_s) * spread(lax.rsqrt(frob))
    gain = jnp.sum(update * spread(pull), axis=1, keepdims=True)
    shift = mean + over_members(update * gain)
    result = spread(shift) + jnp.sqrt(count - 1.0) * update
    for i, ref in enumerate(out_refs):
        ref[...] = result[i * share : (i + 1) * share]


def halves(x):
    return jnp.concatenate(split(x), axis=1)


def folded_product(a, b):
    n = b.shape[1] // 2
    both = jnp.concatenate([b, b], axis=0)
    out = jnp.dot(a, both, preferred_element_type=jnp.float32)
    return out[:, :n] + out[:, n:]


def folded_analysis_kernel(parts, *refs):
    ens_refs, (dsum_ref, vsum_ref) = refs[:parts], refs[parts : parts + 2]
    out_refs = refs[parts + 2 :]
    share, lon = ens_refs[0].shape
    count = share * parts // 8
    size = count * 4

    def low(n):
        return lax.broadcasted_iota(jnp.int32, (8, n), 0) < 4

    def turn(x):
        return pltpu.roll(x, 4, x.ndim - 2)

    def pattern(x):
        r, first = turn(x), low(x.shape[1])
        return jnp.where(first, x, r), jnp.where(first, r, x)

    def spread(x):
        n = x.shape[1]
        return jnp.broadcast_to(x[None], (count // 2, 8, n)).reshape(size, n)

    def over_members(x):
        total = jnp.sum(x.reshape(count // 2, 8, x.shape[1]), axis=0)
        return total + turn(total)

    ens = jnp.concatenate([ref[...] for ref in ens_refs], axis=0).reshape(count, 8, lon)
    dsum = dsum_ref[...]
    mean = jnp.sum(ens, axis=0) * (1.0 / count)
    pert = ens - mean[None]
    turned = turn(pert).reshape(count // 2, 2, 8, lon)
    pert = pert.reshape(count // 2, 2, 8, lon)
    first = low(lon)[None]
    groups = (
        jnp.where(first, pert[:, 0], turned[:, 1]).reshape(size, lon),
        jnp.where(first, turned[:, 0], pert[:, 1]).reshape(size, lon),
    )
    means = pattern(mean)
    dsums = pattern(dsum)
    pulls = pattern(vsum_ref[...] - dsum * mean)

    row = lax.broadcasted_iota(jnp.int32, (size, size), 0)
    col = lax.broadcasted_iota(jnp.int32, (size, size), 1)
    same = lax.rem(row, 4) == lax.rem(col, 4)
    one = jnp.where(row == col, 1.0, 0.0)

    def start(x, dsum):
        high, rest = split(x)
        w_high, w_low = split(x * spread(dsum))
        nt = (((1,), (1,)), ((), ()))
        main = lax.dot_general(
            w_high,
            jnp.concatenate([high, rest], axis=0),
            nt,
            preferred_element_type=jnp.float32,
        )
        more = lax.dot_general(w_low, high, nt, preferred_element_type=jnp.float32)
        gram = main[:, :size] + main[:, size:] + more
        system = jnp.where(same, gram, 0.0) + (count - 1.0) * one
        squares = jnp.sum(system * system, axis=1, keepdims=True)
        frob = jnp.sqrt(over_members(jnp.broadcast_to(squares, (size, size))))
        return system * spread(1.0 / frob), frob, jnp.concatenate([high, rest], axis=1)

    begun = [start(x, d) for x, d in zip(groups, dsums)]
    frobs = [b[1] for b in begun]
    perts = [b[2] for b in begun]
    steps = [b[0] for b in begun]
    iterates = [halves(x) for x in steps]
    inverses = None
    for sweep in range(SWEEPS):
        if inverses is not None:
            steps = [folded_product(z, y) for z, y in zip(inverses, iterates)]
        factors = [halves(1.5 * one - 0.5 * x) for x in steps]
        if sweep == SWEEPS - 1:
            break
        iterates = [halves(folded_product(y, f)) for y, f in zip(iterates, factors)]
        if inverses is None:
            inverses = factors
        else:
            inverses = [halves(folded_product(f, z)) for f, z in zip(factors, inverses)]
    partials = [halves(folded_product(z, x)) for z, x in zip(inverses, perts)]
    results = []
    for factor, part, frob, pull, mean_g in zip(factors, partials, frobs, pulls, means):
        scale = jnp.concatenate([spread(lax.rsqrt(frob))] * (lon // size), axis=1)
        update = folded_product(factor, part) * scale
        gain = jnp.sum(update * spread(pull), axis=1, keepdims=True)
        shift = mean_g + over_members(update * gain)
        results.append(
            (spread(shift) + jnp.sqrt(count - 1.0) * update).reshape(count // 2, 8, lon)
        )
    x, y = results
    even, odd = jnp.where(first, x, turn(y)), jnp.where(first, turn(x), y)
    for i in range(count // 2):
        ref, k = out_refs[2 * i // (share // 8)], (2 * i) % (share // 8)
        ref[8 * k : 8 * k + 8] = even[i]
        ref[8 * k + 8 : 8 * k + 16] = odd[i]


def analysis(ens, dsum, vsum):
    parts = len(ens)
    share, lon = ens[0].shape
    size = share * parts
    regions = dsum.shape[0]
    kernel = functools.partial(analysis_kernel, regions, parts)
    if regions == 8 and size == 256 and lon % 128 == 0 and share % 16 == 0:
        kernel = functools.partial(folded_analysis_kernel, parts)
    return pl.pallas_call(
        kernel,
        out_shape=(jax.ShapeDtypeStruct((share, lon), jnp.float32),) * parts,
        in_specs=whole(parts + 2),
        out_specs=tuple(whole(parts)),
        cost_estimate=pl.CostEstimate(
            flops=48 * size * size * lon, bytes_accessed=8 * size * lon, transcendentals=0
        ),
        compiler_params=SMALL,
        name="analysis",
    )(*ens, dsum, vsum)


def place_rows_kernel(bands, crossed, *refs):
    out_ref, sems = refs[-2:]
    half = out_ref.shape[1] // 2
    got_refs, half_refs = refs[:half], refs[half : 2 * half]
    members = out_ref.shape[0]
    chip, high, at_edge = place(bands)
    copies = []
    for t, ref in enumerate(half_refs):
        mine = row_at(high, 2 * half, row_of(chip, t, crossed))
        other = 2 * half - 1 - mine
        for source, row in ((ref.at[pl.ds(0, members)], mine), (got_refs[t], other)):
            copies.append(
                pltpu.make_async_copy(source, out_ref.at[:, row], sems.at[len(copies)])
            )
    for copy in copies:
        copy.start()
    for copy in copies:
        copy.wait()


def place_rows(bands, crossed, got, halves, shape):
    half = len(halves)
    return pl.pallas_call(
        functools.partial(place_rows_kernel, bands, crossed),
        out_shape=jax.ShapeDtypeStruct(shape, jnp.float32),
        in_specs=whole(2 * half),
        out_specs=pl.BlockSpec(memory_space=pltpu.HBM),
        scratch_shapes=[pltpu.SemaphoreType.DMA((2 * half,))],
        compiler_params=SMALL,
        name="place_rows",
    )(*got, *halves)


def body(state, zonal_wind, meridional_wind, obs_cell, obs_value, obs_weight):
    members, rows, levels, lon = state.shape
    groups = lax.axis_size("member")
    bands = lax.axis_size("lat")
    half = rows // 2
    chips = groups // 2
    regions = half * levels // chips
    crossed = chips == half and chips <= 4 and chips & (chips - 1) == 0

    def grouped(x):
        return x.reshape(groups, regions, x.shape[-1])

    partner = swap(state, groups, 1)
    own, zonal, merid, *tables = stage(
        bands,
        (state, zonal_wind, meridional_wind),
        (grouped(obs_cell), grouped(obs_value), grouped(obs_weight)),
    )
    message = edge_message(bands, own, partner, zonal, merid)
    halo = lax.ppermute(message, ("member", "lat"), halo_pairs(groups, bands))

    dsum, vsum = per_cell(*tables, lon)
    inner, *sent = forecast_inner(bands, crossed, own, partner, zonal, merid)
    sent = forecast_edge(
        bands, crossed, own, partner, halo, zonal, merid, inner, sent, dsum, vsum
    )
    same_core = [list(range(core, groups, 2)) for core in range(2)]

    def exchange(blocks):
        if crossed:
            return [blocks[0]] + [swap(b, groups, 2 * t) for t, b in enumerate(blocks) if t]
        return [
            lax.all_to_all(
                blocks[0], "member", 0, 0, tiled=True, axis_index_groups=same_core
            )
        ]

    if not crossed:
        field = jnp.stack(sent, axis=1).reshape(2 * members, chips, regions, lon)
        sent = [field.transpose(1, 0, 2, 3)]
    ensemble = exchange(sent)
    flat = [x.reshape(-1, lon) for x in ensemble]
    analysed = analysis(flat, dsum, vsum)
    back = exchange([x.reshape(e.shape) for x, e in zip(analysed, ensemble)])
    if not crossed:
        field = back[0].transpose(1, 0, 2, 3).reshape(2 * members, half, levels, lon)
        back = [field[:, t] for t in range(half)]
    got = [swap(b[members:], groups, 1) for b in back]
    return place_rows(bands, crossed, got, back, state.shape)


def solution(mesh):
    in_specs = (
        P("member", "lat", None, None),
        P("lat", None, None),
        P("lat", None, None),
        P("lat", None, None),
        P("lat", None, None),
        P("lat", None, None),
    )
    out_specs = P("member", "lat", None, None)
    return jax.shard_map(body, mesh=mesh, in_specs=in_specs, out_specs=out_specs, check_vma=False)
```

```python
import functools

import jax
import jax.numpy as jnp
from jax import lax
from jax.experimental import pallas as pl
from jax.experimental.pallas import tpu as pltpu
from jax.sharding import PartitionSpec as P

SWEEPS = 3
step_size = 0.3
VM = pltpu.VMEM
SMALL = pltpu.CompilerParams(vmem_limit_bytes=12 * 2**20)


def whole(n):
    return [pl.BlockSpec(memory_space=VM)] * n


def place(bands):
    member, band = lax.axis_index("member"), lax.axis_index("lat")
    core, chip = lax.rem(member, 2), lax.div(member, 2)
    high = lax.rem(core + band, 2) == 0
    at_edge = jnp.where(high, band == bands - 1, band == 0)
    return chip, high, at_edge


def row_at(high, rows, e):
    return jnp.where(high, rows - 1 - e, e)


def halo_pairs(groups, bands):
    pairs = []
    for member in range(groups):
        for band in range(bands):
            other, peer = band + (1 if (member + band) % 2 == 0 else -1), member
            if not 0 <= other < bands:
                other, peer = band, member ^ 2 if groups % 4 == 0 else member
            pairs.append((member * bands + band, peer * bands + other))
    return pairs


def swap(x, groups, distance):
    return lax.ppermute(x, "member", [(i, i ^ distance) for i in range(groups)])


def stage_kernel(bands, *refs):
    sources, targets, sems = refs[:6], refs[6:12], refs[12]
    chip, high, at_edge = place(bands)
    rows, levels = sources[0].shape[1:3]
    per_row = levels // sources[3].shape[1]
    mine = row_at(high, rows, lax.div(chip, per_row)) * per_row + lax.rem(chip, per_row)
    sources = list(sources[:3]) + [ref.at[mine] for ref in sources[3:]]
    copies = [
        pltpu.make_async_copy(source, target, sems.at[i])
        for i, (source, target) in enumerate(zip(sources, targets))
    ]
    for copy in copies:
        copy.start()
    for copy in copies:
        copy.wait()


def stage(bands, fields, tables):
    shapes = [x.shape for x in fields] + [x.shape[1:] for x in tables]
    args = [pltpu.with_memory_space_constraint(x, pltpu.HBM) for x in (*fields, *tables)]
    return pl.pallas_call(
        functools.partial(stage_kernel, bands),
        out_shape=tuple(jax.ShapeDtypeStruct(n, x.dtype) for n, x in zip(shapes, args)),
        in_specs=[pl.BlockSpec(memory_space=pltpu.HBM)] * 6,
        out_specs=tuple(whole(6)),
        scratch_shapes=[pltpu.SemaphoreType.DMA((6,))],
        cost_estimate=pl.CostEstimate(flops=0, bytes_accessed=2**21, transcendentals=0),
        compiler_params=SMALL,
        name="stage",
    )(*args)


def edges_kernel(bands, own_ref, partner_ref, zonal_ref, merid_ref, out_ref):
    members, rows, levels, lon = own_ref.shape
    chip, high, at_edge = place(bands)
    edge = row_at(high, rows, 0)
    for m in range(2 * members):
        ref = own_ref if m < members else partner_ref
        out_ref[2 * m] = ref[m % members, edge]
        out_ref[2 * m + 1] = ref[m % members, row_at(high, rows, 1)]
    out_ref[4 * members] = zonal_ref[edge]
    out_ref[4 * members + 1] = merid_ref[edge]


def edge_message(bands, own, partner, zonal, merid):
    members, rows, levels, lon = own.shape
    return pl.pallas_call(
        functools.partial(edges_kernel, bands),
        out_shape=jax.ShapeDtypeStruct((4 * members + 2, levels, lon), jnp.float32),
        in_specs=whole(4),
        out_specs=pl.BlockSpec(memory_space=VM),
        compiler_params=SMALL,
        name="edges",
    )(own, partner, zonal, merid)


def advance(before, middle, after, zonal, inward):
    lon = middle.shape[-1]
    axis = middle.ndim - 1
    east = pltpu.roll(middle, lon - 1, axis)
    west = pltpu.roll(middle, 1, axis)
    change = (zonal + middle) * (east - west) + inward * (after - before)
    return middle - (0.5 * step_size) * change


def wind_row(high, rows, e, zonal_ref, merid_ref):
    row = row_at(high, rows, e)
    return zonal_ref[row], jnp.where(high, -merid_ref[row], merid_ref[row])


def row_of(chip, t, crossed):
    return lax.bitwise_xor(chip, t) if crossed else t


def inner_kernel(bands, own_ref, partner_ref, zonal_ref, merid_ref, first_ref, done_ref):
    members, rows, levels, lon = own_ref.shape
    half = rows // 2
    chip, high, at_edge = place(bands)
    wind = [wind_row(high, rows, e, zonal_ref, merid_ref) for e in range(1, half + 1)]
    for m in range(2 * members):
        ref, k = (own_ref if m < members else partner_ref), m % members
        q = [ref[k, row_at(high, rows, e)] for e in range(half + 2)]
        for e in range(1, half + 1):
            first_ref[e - 1, m] = advance(q[e - 1], q[e], q[e + 1], *wind[e - 1])
    for e in range(2, half):
        wind = wind_row(high, rows, e, zonal_ref, merid_ref)
        for m in range(2 * members):
            done_ref[e - 2, m] = advance(
                first_ref[e - 2, m], first_ref[e - 1, m], first_ref[e, m], *wind
            )


def edge_kernel(
    bands,
    crossed,
    own_ref,
    partner_ref,
    halo_ref,
    zonal_ref,
    merid_ref,
    inner_ref,
    done_ref,
    dsum_ref,
    vsum_ref,
    *refs,
):
    members, rows, levels, lon = own_ref.shape
    half = rows // 2
    out_refs, edge_ref = refs[:half], refs[half]
    chip, high, at_edge = place(bands)

    def halo(i):
        return jnp.where(at_edge, 0.0, halo_ref[i])

    merid = halo(4 * members + 1)
    outside = halo(4 * members), jnp.where(high, -merid, merid)
    wind = [wind_row(high, rows, e, zonal_ref, merid_ref) for e in range(2)]
    for m in range(2 * members):
        ref, k = (own_ref if m < members else partner_ref), m % members
        q = [halo(2 * m + 1), halo(2 * m)]
        q += [ref[k, row_at(high, rows, e)] for e in range(2)]
        first = [
            advance(q[0], q[1], q[2], *outside),
            advance(q[1], q[2], q[3], *wind[0]),
            inner_ref[0, m],
            inner_ref[1, m],
        ]
        for e in range(2):
            edge_ref[e, m] = advance(first[e], first[e + 1], first[e + 2], *wind[e])
    for t, out_ref in enumerate(out_refs):
        e = row_of(chip, t, crossed)
        if not crossed:
            out_ref[...] = edge_ref[e] if e < 2 else done_ref[e - 2]
            continue
        near, far = jnp.minimum(e, 1), jnp.maximum(e - 2, 0)
        for m in range(2 * members):
            out_ref[m] = jnp.where(e < 2, edge_ref[near, m], done_ref[far, m])


def forecast_inner(bands, own, partner, zonal, merid):
    members, rows, levels, lon = own.shape
    half = rows // 2
    size = own.size
    block = (2 * members, levels, lon)
    return pl.pallas_call(
        functools.partial(inner_kernel, bands),
        out_shape=tuple(
            jax.ShapeDtypeStruct((n, *block), jnp.float32) for n in (half, half - 2)
        ),
        in_specs=whole(4),
        out_specs=tuple(whole(2)),
        cost_estimate=pl.CostEstimate(
            flops=16 * size, bytes_accessed=8 * size, transcendentals=0
        ),
        compiler_params=SMALL,
        name="forecast_inner",
    )(own, partner, zonal, merid)


def forecast_edge(bands, crossed, own, partner, halo, zonal, merid, inner, done, dsum, vsum):
    members, rows, levels, lon = own.shape
    half = rows // 2
    size = own.size
    block = (2 * members, levels, lon)
    return pl.pallas_call(
        functools.partial(edge_kernel, bands, crossed),
        out_shape=(jax.ShapeDtypeStruct(block, jnp.float32),) * half,
        in_specs=whole(7) + [pl.BlockSpec(memory_space=pl.ANY)] * 2,
        out_specs=tuple(whole(half)),
        scratch_shapes=[VM((2, *block), jnp.float32)],
        cost_estimate=pl.CostEstimate(
            flops=8 * size, bytes_accessed=4 * size, transcendentals=0
        ),
        compiler_params=SMALL,
        name="forecast_edge",
    )(own, partner, halo, zonal, merid, inner, done, dsum, vsum)


def cells_kernel(cell_ref, value_ref, weight_ref, dsum_ref, vsum_ref):
    regions, obs = cell_ref.shape
    lon = dsum_ref.shape[1]
    weight = weight_ref[...]
    cell_t = cell_ref[...].T
    weight_t = weight.T
    value_t = (weight * value_ref[...]).T
    index = lax.broadcasted_iota(jnp.int32, (obs, lon), 1)
    for r in range(regions):
        hit = jnp.broadcast_to(cell_t[:, r : r + 1], (obs, lon)) == index
        w = jnp.broadcast_to(weight_t[:, r : r + 1], (obs, lon))
        v = jnp.broadcast_to(value_t[:, r : r + 1], (obs, lon))
        dsum_ref[r : r + 1, :] = jnp.sum(jnp.where(hit, w, 0.0), axis=0, keepdims=True)
        vsum_ref[r : r + 1, :] = jnp.sum(jnp.where(hit, v, 0.0), axis=0, keepdims=True)


def per_cell(cells, values, weights, lon):
    regions, obs = cells.shape
    shape = jax.ShapeDtypeStruct((regions, lon), jnp.float32)
    return pl.pallas_call(
        cells_kernel,
        out_shape=(shape, shape),
        in_specs=whole(3),
        out_specs=tuple(whole(2)),
        cost_estimate=pl.CostEstimate(
            flops=4 * regions * obs * lon,
            bytes_accessed=4 * (3 * regions * obs + 2 * regions * lon),
            transcendentals=0,
        ),
        compiler_params=SMALL,
        name="per_cell",
    )(cells, values, weights)


def split(x):
    high = x.astype(jnp.bfloat16)
    low = (x - high.astype(jnp.float32)).astype(jnp.bfloat16)
    return high, low


def product(a, b, dims=((1,), (0,))):
    def dot(x, y):
        return lax.dot_general(x, y, (dims, ((), ())), preferred_element_type=jnp.float32)

    return dot(a[0], b[0]) + (dot(a[0], b[1]) + dot(a[1], b[0]))


def analysis_kernel(regions, parts, *refs):
    ens_refs, (dsum_ref, vsum_ref) = refs[:parts], refs[parts : parts + 2]
    out_refs = refs[parts + 2 :]
    share, lon = ens_refs[0].shape
    size = share * parts
    count = size // regions

    def over_members(x):
        if regions == 1:
            return jnp.sum(x, axis=0, keepdims=True)
        return jnp.sum(x.reshape(count, regions, x.shape[-1]), axis=0)

    def spread(x):
        if regions == 1:
            return jnp.broadcast_to(x, (size, x.shape[-1]))
        x = jnp.broadcast_to(x[None], (count, regions, x.shape[-1]))
        return x.reshape(size, x.shape[-1])

    ens = jnp.concatenate([ref[...] for ref in ens_refs], axis=0)
    dsum = dsum_ref[...]
    mean = over_members(ens) * (1.0 / count)
    pert = ens - spread(mean)
    pull = vsum_ref[...] - dsum * mean

    row = lax.broadcasted_iota(jnp.int32, (size, size), 0)
    col = lax.broadcasted_iota(jnp.int32, (size, size), 1)
    same = lax.rem(row, regions) == lax.rem(col, regions)
    one = jnp.where(row == col, 1.0, 0.0)

    pert_s = split(pert)
    gram = product(split(pert * spread(dsum)), pert_s, ((1,), (1,)))
    system = jnp.where(same, gram, 0.0) + (count - 1.0) * one
    total = over_members(jnp.sum(system * system, axis=1, keepdims=True))
    frob = jnp.sqrt(total)
    iterate = system * spread(1.0 / frob)
    iterate_s = split(iterate)
    inverse_s = None
    for sweep in range(SWEEPS):
        step = iterate if inverse_s is None else product(inverse_s, iterate_s)
        factor_s = split(1.5 * one - 0.5 * step)
        if sweep == SWEEPS - 1:
            break
        iterate_s = split(product(iterate_s, factor_s))
        inverse_s = factor_s if inverse_s is None else split(product(factor_s, inverse_s))
    part_s = split(product(inverse_s, pert_s))
    update = product(factor_s, part_s) * spread(lax.rsqrt(frob))
    gain = jnp.sum(update * spread(pull), axis=1, keepdims=True)
    shift = mean + over_members(update * gain)
    result = spread(shift) + jnp.sqrt(count - 1.0) * update
    for i, ref in enumerate(out_refs):
        ref[...] = result[i * share : (i + 1) * share]


def halves(x):
    return jnp.concatenate(split(x), axis=1)


def folded_product(a, b):
    n = b.shape[1] // 2
    both = jnp.concatenate([b, b], axis=0)
    out = jnp.dot(a, both, preferred_element_type=jnp.float32)
    return out[:, :n] + out[:, n:]


def folded_analysis_kernel(parts, *refs):
    ens_refs, (dsum_ref, vsum_ref) = refs[:parts], refs[parts : parts + 2]
    out_refs = refs[parts + 2 :]
    share, lon = ens_refs[0].shape
    count = share * parts // 8
    size = count * 4

    def low(n):
        return lax.broadcasted_iota(jnp.int32, (8, n), 0) < 4

    def turn(x):
        return pltpu.roll(x, 4, x.ndim - 2)

    def pattern(x):
        r, first = turn(x), low(x.shape[1])
        return jnp.where(first, x, r), jnp.where(first, r, x)

    def spread(x):
        n = x.shape[1]
        return jnp.broadcast_to(x[None], (count // 2, 8, n)).reshape(size, n)

    def over_members(x):
        total = jnp.sum(x.reshape(count // 2, 8, x.shape[1]), axis=0)
        return total + turn(total)

    ens = jnp.concatenate([ref[...] for ref in ens_refs], axis=0).reshape(count, 8, lon)
    dsum = dsum_ref[...]
    mean = jnp.sum(ens, axis=0) * (1.0 / count)
    pert = ens - mean[None]
    turned = turn(pert).reshape(count // 2, 2, 8, lon)
    pert = pert.reshape(count // 2, 2, 8, lon)
    first = low(lon)[None]
    groups = (
        jnp.where(first, pert[:, 0], turned[:, 1]).reshape(size, lon),
        jnp.where(first, turned[:, 0], pert[:, 1]).reshape(size, lon),
    )
    means = pattern(mean)
    dsums = pattern(dsum)
    pulls = pattern(vsum_ref[...] - dsum * mean)

    row = lax.broadcasted_iota(jnp.int32, (size, size), 0)
    col = lax.broadcasted_iota(jnp.int32, (size, size), 1)
    same = lax.rem(row, 4) == lax.rem(col, 4)
    one = jnp.where(row == col, 1.0, 0.0)

    def start(x, dsum):
        high, rest = split(x)
        w_high, w_low = split(x * spread(dsum))
        nt = (((1,), (1,)), ((), ()))
        main = lax.dot_general(
            w_high,
            jnp.concatenate([high, rest], axis=0),
            nt,
            preferred_element_type=jnp.float32,
        )
        more = lax.dot_general(w_low, high, nt, preferred_element_type=jnp.float32)
        gram = main[:, :size] + main[:, size:] + more
        system = jnp.where(same, gram, 0.0) + (count - 1.0) * one
        system_s = halves(system)
        square = folded_product(system_s, system_s)
        total = jnp.sum(system * system, axis=1, keepdims=True)
        frob = jnp.sqrt(over_members(jnp.broadcast_to(total, (size, size))))
        scale = spread(1.0 / frob)
        iterate = system * scale
        first = 1.5 * iterate - (0.5 * scale) * (square * scale)
        return iterate, first, frob, jnp.concatenate([high, rest], axis=1)

    begun = [start(x, d) for x, d in zip(groups, dsums)]
    frobs = [b[2] for b in begun]
    perts = [b[3] for b in begun]
    inverses = [halves(1.5 * one - 0.5 * b[0]) for b in begun]
    iterates = [halves(b[1]) for b in begun]
    for sweep in range(1, SWEEPS):
        steps = [folded_product(y, z) for z, y in zip(inverses, iterates)]
        factors = [halves(1.5 * one - 0.5 * x) for x in steps]
        if sweep == SWEEPS - 1:
            break
        iterates = [halves(folded_product(f, y)) for y, f in zip(iterates, factors)]
        inverses = [halves(folded_product(f, z)) for f, z in zip(factors, inverses)]
    partials = [halves(folded_product(z, x)) for z, x in zip(inverses, perts)]
    results = []
    for factor, part, frob, pull, mean_g in zip(factors, partials, frobs, pulls, means):
        scale = jnp.concatenate([spread(lax.rsqrt(frob))] * (lon // size), axis=1)
        update = folded_product(factor, part) * scale
        gain = jnp.sum(update * spread(pull), axis=1, keepdims=True)
        shift = mean_g + over_members(update * gain)
        results.append(
            (spread(shift) + jnp.sqrt(count - 1.0) * update).reshape(count // 2, 8, lon)
        )
    x, y = results
    even, odd = jnp.where(first, x, turn(y)), jnp.where(first, turn(x), y)
    for i in range(count // 2):
        ref, k = out_refs[2 * i // (share // 8)], (2 * i) % (share // 8)
        ref[8 * k : 8 * k + 8] = even[i]
        ref[8 * k + 8 : 8 * k + 16] = odd[i]


def analysis(ens, dsum, vsum):
    parts = len(ens)
    share, lon = ens[0].shape
    size = share * parts
    regions = dsum.shape[0]
    kernel = functools.partial(analysis_kernel, regions, parts)
    if regions == 8 and size == 256 and lon % 128 == 0 and share % 16 == 0:
        kernel = functools.partial(folded_analysis_kernel, parts)
    return pl.pallas_call(
        kernel,
        out_shape=(jax.ShapeDtypeStruct((share, lon), jnp.float32),) * parts,
        in_specs=whole(parts + 2),
        out_specs=tuple(whole(parts)),
        cost_estimate=pl.CostEstimate(
            flops=48 * size * size * lon, bytes_accessed=8 * size * lon, transcendentals=0
        ),
        compiler_params=SMALL,
        name="analysis",
    )(*ens, dsum, vsum)


def place_rows_kernel(bands, crossed, *refs):
    out_ref, sems = refs[-2:]
    half = out_ref.shape[1] // 2
    got_refs, half_refs = refs[:half], refs[half : 2 * half]
    members = out_ref.shape[0]
    chip, high, at_edge = place(bands)
    copies = []
    for t, ref in enumerate(half_refs):
        mine = row_at(high, 2 * half, row_of(chip, t, crossed))
        other = 2 * half - 1 - mine
        for source, row in ((ref.at[pl.ds(0, members)], mine), (got_refs[t], other)):
            copies.append(
                pltpu.make_async_copy(source, out_ref.at[:, row], sems.at[len(copies)])
            )
    for copy in copies:
        copy.start()
    for copy in copies:
        copy.wait()


def place_rows(bands, crossed, got, halves, shape):
    half = len(halves)
    return pl.pallas_call(
        functools.partial(place_rows_kernel, bands, crossed),
        out_shape=jax.ShapeDtypeStruct(shape, jnp.float32),
        in_specs=whole(2 * half),
        out_specs=pl.BlockSpec(memory_space=pltpu.HBM),
        scratch_shapes=[pltpu.SemaphoreType.DMA((2 * half,))],
        compiler_params=SMALL,
        name="place_rows",
    )(*got, *halves)


def body(state, zonal_wind, meridional_wind, obs_cell, obs_value, obs_weight):
    members, rows, levels, lon = state.shape
    groups = lax.axis_size("member")
    bands = lax.axis_size("lat")
    half = rows // 2
    chips = groups // 2
    regions = half * levels // chips
    crossed = chips == half and chips <= 4 and chips & (chips - 1) == 0

    def grouped(x):
        return x.reshape(groups, regions, x.shape[-1])

    partner = swap(state, groups, 1)
    own, zonal, merid, *tables = stage(
        bands,
        (state, zonal_wind, meridional_wind),
        (grouped(obs_cell), grouped(obs_value), grouped(obs_weight)),
    )
    message = edge_message(bands, own, partner, zonal, merid)
    halo = lax.ppermute(message, ("member", "lat"), halo_pairs(groups, bands))

    dsum, vsum = per_cell(*tables, lon)
    inner, done = forecast_inner(bands, own, partner, zonal, merid)
    sent = forecast_edge(
        bands, crossed, own, partner, halo, zonal, merid, inner, done, dsum, vsum
    )
    same_core = [list(range(core, groups, 2)) for core in range(2)]

    def exchange(blocks):
        if crossed:
            return [blocks[0]] + [swap(b, groups, 2 * t) for t, b in enumerate(blocks) if t]
        return [
            lax.all_to_all(
                blocks[0], "member", 0, 0, tiled=True, axis_index_groups=same_core
            )
        ]

    if not crossed:
        field = jnp.stack(sent, axis=1).reshape(2 * members, chips, regions, lon)
        sent = [field.transpose(1, 0, 2, 3)]
    ensemble = exchange(sent)
    flat = [x.reshape(-1, lon) for x in ensemble]
    analysed = analysis(flat, dsum, vsum)
    back = exchange([x.reshape(e.shape) for x, e in zip(analysed, ensemble)])
    if not crossed:
        field = back[0].transpose(1, 0, 2, 3).reshape(2 * members, half, levels, lon)
        back = [field[:, t] for t in range(half)]
    got = [swap(b[members:], groups, 1) for b in back]
    return place_rows(bands, crossed, got, back, state.shape)


def solution(mesh):
    in_specs = (
        P("member", "lat", None, None),
        P("lat", None, None),
        P("lat", None, None),
        P("lat", None, None),
        P("lat", None, None),
        P("lat", None, None),
    )
    out_specs = P("member", "lat", None, None)
    return jax.shard_map(body, mesh=mesh, in_specs=in_specs, out_specs=out_specs, check_vma=False)
```

```python
import functools

import jax
import jax.numpy as jnp
from jax import lax
from jax.experimental import pallas as pl
from jax.experimental.pallas import tpu as pltpu
from jax.sharding import PartitionSpec as P

SWEEPS = 3
step_size = 0.3
VM = pltpu.VMEM
SMALL = pltpu.CompilerParams(vmem_limit_bytes=12 * 2**20)


def whole(n):
    return [pl.BlockSpec(memory_space=VM)] * n


def place(bands):
    member, band = lax.axis_index("member"), lax.axis_index("lat")
    core, chip = lax.rem(member, 2), lax.div(member, 2)
    high = lax.rem(core + band, 2) == 0
    at_edge = jnp.where(high, band == bands - 1, band == 0)
    return chip, high, at_edge


def row_at(high, rows, e):
    return jnp.where(high, rows - 1 - e, e)


def halo_pairs(groups, bands):
    pairs = []
    for member in range(groups):
        for band in range(bands):
            other, peer = band + (1 if (member + band) % 2 == 0 else -1), member
            if not 0 <= other < bands:
                other, peer = band, member ^ 2 if groups % 4 == 0 else member
            pairs.append((member * bands + band, peer * bands + other))
    return pairs


def swap(x, groups, distance):
    return lax.ppermute(x, "member", [(i, i ^ distance) for i in range(groups)])


def stage_kernel(bands, *refs):
    sources, targets, sems = refs[:6], refs[6:12], refs[12]
    chip, high, _ = place(bands)
    rows, levels = sources[0].shape[1:3]
    per_row = levels // sources[3].shape[1]
    mine = row_at(high, rows, lax.div(chip, per_row)) * per_row + lax.rem(chip, per_row)
    sources = list(sources[:3]) + [ref.at[mine] for ref in sources[3:]]
    copies = [
        pltpu.make_async_copy(source, target, sems.at[i])
        for i, (source, target) in enumerate(zip(sources, targets))
    ]
    for copy in copies:
        copy.start()
    for copy in copies:
        copy.wait()


def stage(bands, fields, tables):
    shapes = [x.shape for x in fields] + [x.shape[1:] for x in tables]
    args = [pltpu.with_memory_space_constraint(x, pltpu.HBM) for x in (*fields, *tables)]
    return pl.pallas_call(
        functools.partial(stage_kernel, bands),
        out_shape=tuple(jax.ShapeDtypeStruct(n, x.dtype) for n, x in zip(shapes, args)),
        in_specs=[pl.BlockSpec(memory_space=pltpu.HBM)] * 6,
        out_specs=tuple(whole(6)),
        scratch_shapes=[pltpu.SemaphoreType.DMA((6,))],
        cost_estimate=pl.CostEstimate(flops=0, bytes_accessed=2**21, transcendentals=0),
        compiler_params=SMALL,
        name="stage",
    )(*args)


def edges_kernel(bands, own_ref, partner_ref, zonal_ref, merid_ref, out_ref):
    members, rows, _, _ = own_ref.shape
    _, high, _ = place(bands)
    edge = row_at(high, rows, 0)
    for m in range(2 * members):
        ref = own_ref if m < members else partner_ref
        out_ref[2 * m] = ref[m % members, edge]
        out_ref[2 * m + 1] = ref[m % members, row_at(high, rows, 1)]
    out_ref[4 * members] = zonal_ref[edge]
    out_ref[4 * members + 1] = merid_ref[edge]


def edge_message(bands, own, partner, zonal, merid):
    members, _, levels, lon = own.shape
    return pl.pallas_call(
        functools.partial(edges_kernel, bands),
        out_shape=jax.ShapeDtypeStruct((4 * members + 2, levels, lon), jnp.float32),
        in_specs=whole(4),
        out_specs=pl.BlockSpec(memory_space=VM),
        compiler_params=SMALL,
        name="edges",
    )(own, partner, zonal, merid)


def advance(before, middle, after, zonal, inward):
    lon = middle.shape[-1]
    axis = middle.ndim - 1
    east = pltpu.roll(middle, lon - 1, axis)
    west = pltpu.roll(middle, 1, axis)
    change = (zonal + middle) * (east - west) + inward * (after - before)
    return middle - (0.5 * step_size) * change


def wind_row(high, rows, e, zonal_ref, merid_ref):
    row = row_at(high, rows, e)
    return zonal_ref[row], jnp.where(high, -merid_ref[row], merid_ref[row])


def row_of(chip, t, crossed):
    return lax.bitwise_xor(chip, t) if crossed else t


def inner_kernel(bands, own_ref, partner_ref, zonal_ref, merid_ref, first_ref, done_ref):
    members, rows, _, _ = own_ref.shape
    half = rows // 2
    _, high, _ = place(bands)
    wind = [wind_row(high, rows, e, zonal_ref, merid_ref) for e in range(1, half + 1)]
    for m in range(2 * members):
        ref, k = (own_ref if m < members else partner_ref), m % members
        q = [ref[k, row_at(high, rows, e)] for e in range(half + 2)]
        for e in range(1, half + 1):
            first_ref[e - 1, m] = advance(q[e - 1], q[e], q[e + 1], *wind[e - 1])
    for e in range(2, half):
        wind = wind_row(high, rows, e, zonal_ref, merid_ref)
        for m in range(2 * members):
            done_ref[e - 2, m] = advance(
                first_ref[e - 2, m], first_ref[e - 1, m], first_ref[e, m], *wind
            )


def edge_kernel(
    bands,
    crossed,
    own_ref,
    partner_ref,
    halo_ref,
    zonal_ref,
    merid_ref,
    inner_ref,
    done_ref,
    dsum_ref,
    vsum_ref,
    *refs,
):
    members, rows, _, _ = own_ref.shape
    half = rows // 2
    out_refs, edge_ref = refs[:half], refs[half]
    chip, high, at_edge = place(bands)

    def halo(i):
        return jnp.where(at_edge, 0.0, halo_ref[i])

    merid = halo(4 * members + 1)
    outside = halo(4 * members), jnp.where(high, -merid, merid)
    wind = [wind_row(high, rows, e, zonal_ref, merid_ref) for e in range(2)]
    for m in range(2 * members):
        ref, k = (own_ref if m < members else partner_ref), m % members
        q = [halo(2 * m + 1), halo(2 * m)]
        q += [ref[k, row_at(high, rows, e)] for e in range(2)]
        first = [
            advance(q[0], q[1], q[2], *outside),
            advance(q[1], q[2], q[3], *wind[0]),
            inner_ref[0, m],
            inner_ref[1, m],
        ]
        for e in range(2):
            edge_ref[e, m] = advance(first[e], first[e + 1], first[e + 2], *wind[e])
    for t, out_ref in enumerate(out_refs):
        e = row_of(chip, t, crossed)
        if not crossed:
            out_ref[...] = edge_ref[e] if e < 2 else done_ref[e - 2]
            continue
        near, far = jnp.minimum(e, 1), jnp.maximum(e - 2, 0)
        for m in range(2 * members):
            out_ref[m] = jnp.where(e < 2, edge_ref[near, m], done_ref[far, m])


def forecast_inner(bands, own, partner, zonal, merid):
    members, rows, levels, lon = own.shape
    half = rows // 2
    size = own.size
    block = (2 * members, levels, lon)
    return pl.pallas_call(
        functools.partial(inner_kernel, bands),
        out_shape=tuple(
            jax.ShapeDtypeStruct((n, *block), jnp.float32) for n in (half, half - 2)
        ),
        in_specs=whole(4),
        out_specs=tuple(whole(2)),
        cost_estimate=pl.CostEstimate(
            flops=16 * size, bytes_accessed=8 * size, transcendentals=0
        ),
        compiler_params=SMALL,
        name="forecast_inner",
    )(own, partner, zonal, merid)


def forecast_edge(bands, crossed, own, partner, halo, zonal, merid, inner, done, dsum, vsum):
    members, rows, levels, lon = own.shape
    half = rows // 2
    size = own.size
    block = (2 * members, levels, lon)
    return pl.pallas_call(
        functools.partial(edge_kernel, bands, crossed),
        out_shape=(jax.ShapeDtypeStruct(block, jnp.float32),) * half,
        in_specs=whole(7) + [pl.BlockSpec(memory_space=pl.ANY)] * 2,
        out_specs=tuple(whole(half)),
        scratch_shapes=[VM((2, *block), jnp.float32)],
        cost_estimate=pl.CostEstimate(
            flops=8 * size, bytes_accessed=4 * size, transcendentals=0
        ),
        compiler_params=SMALL,
        name="forecast_edge",
    )(own, partner, halo, zonal, merid, inner, done, dsum, vsum)


def cells_kernel(cell_ref, value_ref, weight_ref, dsum_ref, vsum_ref):
    regions, obs = cell_ref.shape
    lon = dsum_ref.shape[1]
    weight = weight_ref[...]
    cell_t = cell_ref[...].T
    weight_t = weight.T
    value_t = (weight * value_ref[...]).T
    index = lax.broadcasted_iota(jnp.int32, (obs, lon), 1)
    for r in range(regions):
        hit = jnp.broadcast_to(cell_t[:, r : r + 1], (obs, lon)) == index
        w = jnp.broadcast_to(weight_t[:, r : r + 1], (obs, lon))
        v = jnp.broadcast_to(value_t[:, r : r + 1], (obs, lon))
        dsum_ref[r : r + 1, :] = jnp.sum(jnp.where(hit, w, 0.0), axis=0, keepdims=True)
        vsum_ref[r : r + 1, :] = jnp.sum(jnp.where(hit, v, 0.0), axis=0, keepdims=True)


def per_cell(cells, values, weights, lon):
    regions, obs = cells.shape
    shape = jax.ShapeDtypeStruct((regions, lon), jnp.float32)
    return pl.pallas_call(
        cells_kernel,
        out_shape=(shape, shape),
        in_specs=whole(3),
        out_specs=tuple(whole(2)),
        cost_estimate=pl.CostEstimate(
            flops=4 * regions * obs * lon,
            bytes_accessed=4 * (3 * regions * obs + 2 * regions * lon),
            transcendentals=0,
        ),
        compiler_params=SMALL,
        name="per_cell",
    )(cells, values, weights)


def split(x):
    high = x.astype(jnp.bfloat16)
    low = (x - high.astype(jnp.float32)).astype(jnp.bfloat16)
    return high, low


def product(a, b, dims=((1,), (0,))):
    def dot(x, y):
        return lax.dot_general(x, y, (dims, ((), ())), preferred_element_type=jnp.float32)

    return dot(a[0], b[0]) + (dot(a[0], b[1]) + dot(a[1], b[0]))


def analysis_kernel(regions, parts, *refs):
    ens_refs, (dsum_ref, vsum_ref) = refs[:parts], refs[parts : parts + 2]
    out_refs = refs[parts + 2 :]
    share, _ = ens_refs[0].shape
    size = share * parts
    count = size // regions

    def over_members(x):
        if regions == 1:
            return jnp.sum(x, axis=0, keepdims=True)
        return jnp.sum(x.reshape(count, regions, x.shape[-1]), axis=0)

    def spread(x):
        if regions == 1:
            return jnp.broadcast_to(x, (size, x.shape[-1]))
        x = jnp.broadcast_to(x[None], (count, regions, x.shape[-1]))
        return x.reshape(size, x.shape[-1])

    ens = jnp.concatenate([ref[...] for ref in ens_refs], axis=0)
    dsum = dsum_ref[...]
    mean = over_members(ens) * (1.0 / count)
    pert = ens - spread(mean)
    pull = vsum_ref[...] - dsum * mean

    row = lax.broadcasted_iota(jnp.int32, (size, size), 0)
    col = lax.broadcasted_iota(jnp.int32, (size, size), 1)
    same = lax.rem(row, regions) == lax.rem(col, regions)
    one = jnp.where(row == col, 1.0, 0.0)

    pert_s = split(pert)
    gram = product(split(pert * spread(dsum)), pert_s, ((1,), (1,)))
    system = jnp.where(same, gram, 0.0) + (count - 1.0) * one
    total = over_members(jnp.sum(system * system, axis=1, keepdims=True))
    frob = jnp.sqrt(total)
    iterate = system * spread(1.0 / frob)
    iterate_s = split(iterate)
    inverse_s = None
    for sweep in range(SWEEPS):
        step = iterate if inverse_s is None else product(inverse_s, iterate_s)
        factor_s = split(1.5 * one - 0.5 * step)
        if sweep == SWEEPS - 1:
            break
        iterate_s = split(product(iterate_s, factor_s))
        inverse_s = factor_s if inverse_s is None else split(product(factor_s, inverse_s))
    part_s = split(product(inverse_s, pert_s))
    update = product(factor_s, part_s) * spread(lax.rsqrt(frob))
    gain = jnp.sum(update * spread(pull), axis=1, keepdims=True)
    shift = mean + over_members(update * gain)
    result = spread(shift) + jnp.sqrt(count - 1.0) * update
    for i, ref in enumerate(out_refs):
        ref[...] = result[i * share : (i + 1) * share]


def halves(x):
    return jnp.concatenate(split(x), axis=1)


def folded_product(a, b):
    n = b.shape[1] // 2
    both = jnp.concatenate([b, b], axis=0)
    out = jnp.dot(a, both, preferred_element_type=jnp.float32)
    return out[:, :n] + out[:, n:]


def folded_analysis_kernel(parts, *refs):
    ens_refs, (dsum_ref, vsum_ref) = refs[:parts], refs[parts : parts + 2]
    out_refs = refs[parts + 2 :]
    share, lon = ens_refs[0].shape
    count = share * parts // 8
    size = count * 4

    def low(n):
        return lax.broadcasted_iota(jnp.int32, (8, n), 0) < 4

    def turn(x):
        return pltpu.roll(x, 4, x.ndim - 2)

    def pattern(x):
        r, first = turn(x), low(x.shape[1])
        return jnp.where(first, x, r), jnp.where(first, r, x)

    def spread(x):
        n = x.shape[1]
        return jnp.broadcast_to(x[None], (count // 2, 8, n)).reshape(size, n)

    def over_members(x):
        total = jnp.sum(x.reshape(count // 2, 8, x.shape[1]), axis=0)
        return total + turn(total)

    ens = jnp.concatenate([ref[...] for ref in ens_refs], axis=0).reshape(count, 8, lon)
    dsum = dsum_ref[...]
    mean = jnp.sum(ens, axis=0) * (1.0 / count)
    pert = ens - mean[None]
    turned = turn(pert).reshape(count // 2, 2, 8, lon)
    pert = pert.reshape(count // 2, 2, 8, lon)
    first = low(lon)[None]
    groups = (
        jnp.where(first, pert[:, 0], turned[:, 1]).reshape(size, lon),
        jnp.where(first, turned[:, 0], pert[:, 1]).reshape(size, lon),
    )
    means = pattern(mean)
    dsums = pattern(dsum)
    pulls = pattern(vsum_ref[...] - dsum * mean)

    row = lax.broadcasted_iota(jnp.int32, (size, size), 0)
    col = lax.broadcasted_iota(jnp.int32, (size, size), 1)
    same = lax.rem(row, 4) == lax.rem(col, 4)
    one = jnp.where(row == col, 1.0, 0.0)

    def start(x, dsum):
        high, rest = split(x)
        w_high, w_low = split(x * spread(dsum))
        nt = (((1,), (1,)), ((), ()))
        main = lax.dot_general(
            w_high,
            jnp.concatenate([high, rest], axis=0),
            nt,
            preferred_element_type=jnp.float32,
        )
        more = lax.dot_general(w_low, high, nt, preferred_element_type=jnp.float32)
        gram = main[:, :size] + main[:, size:] + more
        system = jnp.where(same, gram, 0.0) + (count - 1.0) * one
        system_s = halves(system)
        square = folded_product(system_s, system_s)
        total = jnp.sum(system * system, axis=1, keepdims=True)
        frob = jnp.sqrt(over_members(jnp.broadcast_to(total, (size, size))))
        scale = spread(1.0 / frob)
        iterate = system * scale
        first = 1.5 * iterate - (0.5 * scale) * (square * scale)
        return iterate, first, frob, jnp.concatenate([high, rest], axis=1)

    begun = [start(x, d) for x, d in zip(groups, dsums)]
    frobs = [b[2] for b in begun]
    perts = [b[3] for b in begun]
    inverses = [halves(1.5 * one - 0.5 * b[0]) for b in begun]
    iterates = [halves(b[1]) for b in begun]
    for sweep in range(1, SWEEPS):
        steps = [folded_product(y, z) for z, y in zip(inverses, iterates)]
        factors = [halves(1.5 * one - 0.5 * x) for x in steps]
        if sweep == SWEEPS - 1:
            break
        iterates = [halves(folded_product(f, y)) for y, f in zip(iterates, factors)]
        inverses = [halves(folded_product(f, z)) for f, z in zip(factors, inverses)]
    partials = [halves(folded_product(z, x)) for z, x in zip(inverses, perts)]
    results = []
    for factor, part, frob, pull, mean_g in zip(factors, partials, frobs, pulls, means):
        scale = jnp.concatenate([spread(lax.rsqrt(frob))] * (lon // size), axis=1)
        update = folded_product(factor, part) * scale
        gain = jnp.sum(update * spread(pull), axis=1, keepdims=True)
        shift = mean_g + over_members(update * gain)
        results.append(
            (spread(shift) + jnp.sqrt(count - 1.0) * update).reshape(count // 2, 8, lon)
        )
    x, y = results
    even, odd = jnp.where(first, x, turn(y)), jnp.where(first, turn(x), y)
    for i in range(count // 2):
        ref, k = out_refs[2 * i // (share // 8)], (2 * i) % (share // 8)
        ref[8 * k : 8 * k + 8] = even[i]
        ref[8 * k + 8 : 8 * k + 16] = odd[i]


def analysis(ens, dsum, vsum):
    parts = len(ens)
    share, lon = ens[0].shape
    size = share * parts
    regions = dsum.shape[0]
    kernel = functools.partial(analysis_kernel, regions, parts)
    if regions == 8 and size == 256 and lon % 128 == 0 and share % 16 == 0:
        kernel = functools.partial(folded_analysis_kernel, parts)
    return pl.pallas_call(
        kernel,
        out_shape=(jax.ShapeDtypeStruct((share, lon), jnp.float32),) * parts,
        in_specs=whole(parts + 2),
        out_specs=tuple(whole(parts)),
        cost_estimate=pl.CostEstimate(
            flops=48 * size * size * lon, bytes_accessed=8 * size * lon, transcendentals=0
        ),
        compiler_params=SMALL,
        name="analysis",
    )(*ens, dsum, vsum)


def place_rows_kernel(bands, crossed, *refs):
    out_ref, sems = refs[-2:]
    half = out_ref.shape[1] // 2
    got_refs, half_refs = refs[:half], refs[half : 2 * half]
    members = out_ref.shape[0]
    chip, high, _ = place(bands)
    copies = []
    for t, ref in enumerate(half_refs):
        mine = row_at(high, 2 * half, row_of(chip, t, crossed))
        other = 2 * half - 1 - mine
        for source, row in ((ref.at[pl.ds(0, members)], mine), (got_refs[t], other)):
            copies.append(
                pltpu.make_async_copy(source, out_ref.at[:, row], sems.at[len(copies)])
            )
    for copy in copies:
        copy.start()
    for copy in copies:
        copy.wait()


def place_rows(bands, crossed, got, halves, shape):
    half = len(halves)
    return pl.pallas_call(
        functools.partial(place_rows_kernel, bands, crossed),
        out_shape=jax.ShapeDtypeStruct(shape, jnp.float32),
        in_specs=whole(2 * half),
        out_specs=pl.BlockSpec(memory_space=pltpu.HBM),
        scratch_shapes=[pltpu.SemaphoreType.DMA((2 * half,))],
        compiler_params=SMALL,
        name="place_rows",
    )(*got, *halves)


def body(state, zonal_wind, meridional_wind, obs_cell, obs_value, obs_weight):
    members, rows, levels, lon = state.shape
    groups = lax.axis_size("member")
    bands = lax.axis_size("lat")
    half = rows // 2
    chips = groups // 2
    regions = half * levels // chips
    crossed = chips == half and chips <= 4 and chips & (chips - 1) == 0

    def grouped(x):
        return x.reshape(groups, regions, x.shape[-1])

    partner = swap(state, groups, 1)
    own, zonal, merid, *tables = stage(
        bands,
        (state, zonal_wind, meridional_wind),
        (grouped(obs_cell), grouped(obs_value), grouped(obs_weight)),
    )
    message = edge_message(bands, own, partner, zonal, merid)
    halo = lax.ppermute(message, ("member", "lat"), halo_pairs(groups, bands))

    dsum, vsum = per_cell(*tables, lon)
    inner, done = forecast_inner(bands, own, partner, zonal, merid)
    sent = forecast_edge(
        bands, crossed, own, partner, halo, zonal, merid, inner, done, dsum, vsum
    )
    same_core = [list(range(core, groups, 2)) for core in range(2)]

    def exchange(blocks):
        if crossed:
            moved = [blocks[0]]
            for t in range(1, chips):
                moved.append(swap(blocks[t], groups, 2 * t))
            return moved
        return [
            lax.all_to_all(
                blocks[0], "member", 0, 0, tiled=True, axis_index_groups=same_core
            )
        ]

    if not crossed:
        field = jnp.stack(sent, axis=1).reshape(2 * members, chips, regions, lon)
        sent = [field.transpose(1, 0, 2, 3)]
    ensemble = exchange(sent)
    flat = [x.reshape(-1, lon) for x in ensemble]
    analysed = analysis(flat, dsum, vsum)
    back = exchange([x.reshape(e.shape) for x, e in zip(analysed, ensemble)])
    if not crossed:
        field = back[0].transpose(1, 0, 2, 3).reshape(2 * members, half, levels, lon)
        back = [field[:, t] for t in range(half)]
    got = []
    for block in back:
        got.append(swap(block[members:], groups, 1))
    return place_rows(bands, crossed, got, back, state.shape)


def solution(mesh):
    in_specs = (
        P("member", "lat", None, None),
        P("lat", None, None),
        P("lat", None, None),
        P("lat", None, None),
        P("lat", None, None),
        P("lat", None, None),
    )
    out_specs = P("member", "lat", None, None)

    return jax.shard_map(body, mesh=mesh, in_specs=in_specs, out_specs=out_specs, check_vma=False)
```
